512 devices in a mesh: shot: 32 (over z, x_lo, core), dom: 16 (over y, x_hi).
Axes of the slice: x: 4 (x_hi: 2, x_lo: 2; x = x_hi * 2 + x_lo), y: 8, z: 8, core: 2. Of those that a mesh axis runs over, the one named last changes fastest.
Arguments:
- kappa: float32 [32, 512, 128], P('dom'), may hold values from 0.05 to 0.15
- wave_now: float32 [32, 32, 512, 128], P('shot', 'dom'), may hold values from -6 to 6
- wave_before: float32 [32, 32, 512, 128], P('shot', 'dom'), may hold values from -6 to 6
- wavelet: float32 [32, 4], P('shot'), may hold values from -8 to 8
- source_cell: int32 [32], P('shot'), may hold values from 0 to 2097151
- receiver_cells: int32 [32, 2048], P('shot'), may hold values from 0 to 2097151
- observed: float32 [32, 4, 2048], P('shot'), may hold values from -6 to 6
Outputs:
- total_gradient: float32 [32, 512, 128], P('dom', 'shot')
- wave_next: float32 [32, 32, 512, 128], P('shot', 'dom')
The draws below stay inside these ranges and needn't reach their ends.
Inputs may be any that keep to these rules, and one draw needn't show every extreme that they name: `source_cell`: a cell index x * 512 * 128 + y * 128 + z. `receiver_cells`: cell indices x * 512 * 128 + y * 128 + z; a cell may hold several receivers.
All inputs are finite; a program needn't handle non-finite values.
Results may differ from the reference program's by a relative error of at most 0.00013.
Values sent between devices are 32-bit elements; how exact they have to be, the bound alone decides.
A program may use at most 64 MiB of HBM per device.

```python
import jax
import jax.numpy as jnp
from jax import lax

NY = 512
NZ = 128
NREC = 2048
NT = 4
NX = 32
SHOTS = 32


def plant(array, key, smallest, largest):
    dims = array.shape
    spot = [jax.random.randint(jax.random.fold_in(key, axis), (), 0, dims[axis]) for axis in range(len(dims))]
    array = array.at[tuple(spot)].set(smallest)
    longest = dims.index(max(dims))
    spot[longest] = (spot[longest] + 1) % dims[longest]
    return array.at[tuple(spot)].set(largest)


def levels(own_key, dims, cuts, least, high):
    gain = 1.0
    for dim, shards_of in cuts:
        heights = jax.random.uniform(jax.random.fold_in(jax.random.fold_in(own_key, 6), dim), (shards_of,), jnp.float32, least / len(cuts), high / len(cuts))
        gain = gain * jnp.repeat(jnp.exp(heights), dims[dim] // shards_of).reshape((-1,) + (1,) * (len(dims) - 1 - dim))
    return gain


def gaussian(own_key, extent, spread, most, cuts=(), held_as=jnp.bfloat16):
    drawn = jax.random.normal(own_key, extent, jnp.float32) * spread
    if len(cuts) > 0:
        drawn = levels(own_key, extent, cuts, -0.22, 0.18) * drawn
    return jnp.clip(drawn, min=-most, max=most).astype(held_as)


def setup_inputs(seed: int = 0) -> dict:
    arg_keys = jax.random.split(jax.random.key(seed), 8)
    kappa = jnp.clip(0.05 + 0.10000001 * jax.random.uniform(arg_keys[0], (NX, NY, NZ), jnp.float32) ** levels(arg_keys[0], (NX, NY, NZ), ((0, 16),), -0.2, 0.2), 0.05, 0.15)
    wave_now = gaussian(arg_keys[1], (SHOTS, NX, NY, NZ), 1.0, 6.0, ((0, 32), (1, 16)), jnp.float32)
    wave_before = gaussian(arg_keys[2], (SHOTS, NX, NY, NZ), 1.0, 6.0, ((0, 32), (1, 16)), jnp.float32)
    wavelet = gaussian(arg_keys[3], (SHOTS, NT), 2.0, 8.0, ((0, 32),), jnp.float32)
    source_cell = plant(jax.random.randint(arg_keys[4], (SHOTS,), 0, NX * NY * NZ), jax.random.fold_in(arg_keys[4], 1), 0, (NX * NY * NZ) - 1).astype(jnp.int32)
    receiver_cells = plant(jax.random.randint(arg_keys[5], (SHOTS, NREC), 0, NX * NY * NZ), jax.random.fold_in(arg_keys[5], 1), 0, (NX * NY * NZ) - 1).astype(jnp.int32)
    observed = gaussian(arg_keys[6], (SHOTS, NT, NREC), 1.0, 6.0, ((0, 32),), jnp.float32)
    return {"kappa": kappa, "wave_now": wave_now, "wave_before": wave_before, "wavelet": wavelet, "source_cell": source_cell, "receiver_cells": receiver_cells, "observed": observed}


PRIOR_GAIN = 50.0

def neighbours(padded):
    core = padded[..., 1:-1, :, :]
    widths = [(0, 0)] * (core.ndim - 2) + [(1, 1), (1, 1)]
    flank = jnp.pad(core, widths)
    total = padded[..., 2:, :, :] + padded[..., :-2, :, :]
    total = total + flank[..., 2:, 1:-1] + flank[..., :-2, 1:-1]
    total = total + flank[..., 1:-1, 2:] + flank[..., 1:-1, :-2]
    return total

def laplace(field):
    padded = jnp.pad(field, ((1, 1), (0, 0), (0, 0)))
    return neighbours(padded) - 6.0 * field

def reference(kappa, wave_now, wave_before, wavelet, source_cell, receiver_cells, observed):

    def one_shot(total, items):
        start_now, start_before, pulse, source, receivers, recorded = items

        def misfit(model):
            now, before = (start_now, start_before)
            value = jnp.zeros((), model.dtype)
            for step in range(NT):
                lap = laplace(now)
                after = 2.0 * now - before + model * lap
                after = after.reshape(-1).at[source].add(pulse[step]).reshape(now.shape)
                miss = after.reshape(-1)[receivers] - recorded[step]
                value = value + 0.5 * jnp.sum(miss * miss)
                before, now = (now, after)
            return (value, now)
        value, pull, final = jax.vjp(misfit, kappa, has_aux=True)
        image, = pull(jnp.ones_like(value))
        return (total + image, final)
    image, wave_next = lax.scan(one_shot, jnp.zeros_like(kappa), (wave_now, wave_before, wavelet, source_cell, receiver_cells, observed))
    padded_model = jnp.pad(kappa, ((1, 1), (0, 0), (0, 0)))
    smooth = neighbours(padded_model) / 6.0
    score = (smooth - kappa) * PRIOR_GAIN
    total_gradient = image / NT - score
    return (total_gradient, wave_next)
```

```python
import jax
import jax.numpy as jnp
from jax import lax
from jax.experimental import pallas as pl
from jax.experimental.pallas import tpu as pltpu
from jax.sharding import PartitionSpec as P


NT = 4
PRIOR_GAIN = 50.0
PLANES = 4
ROWS = 264
SHIFT = 248
PAD = 8
BLOCK = 24
CHUNKS = ((0, 96), (96, 96), (192, 72))
CELL_ROWS = PLANES * ROWS
TILE = 352
COLUMNS = 9 * 128
MESH = pl.DeviceIdType.MESH


def kernel(
    kappa_ref, now_ref, before_ref, wavelet_ref, source_ref, receiver_ref, observed_ref,
    gradient_ref, next_ref,
    u, model, source, laps, counts, adjoint, weighted, halo, image,
    onehot_rows, onehot_lanes, kappa_rows, kappa_rim, mate, summed, landed,
    local_sem, pair_send, pair_recv, rim_send, rim_recv, halo_send, halo_recv,
    next_sem, core_send, core_recv, band_send, band_recv,
):
    shot = lax.axis_index("shot")
    dom = lax.axis_index("dom")
    h = lax.rem(dom, 2)
    slab = dom // 2
    core = lax.rem(shot, 2)
    x_lo = lax.rem(shot // 2, 2)
    z = shot // 4
    pair = (shot, dom + 1 - 2 * h)
    above = (shot, lax.rem(dom + 2, 16))
    below = (shot, lax.rem(dom + 14, 16))
    next_dom = (shot, lax.rem(dom + 1, 16))
    last_dom = (shot, lax.rem(dom + 15, 16))
    other = (shot, lax.rem(dom + 15 + 2 * h, 16))
    twin = (shot + 1 - 2 * core, dom)
    in_half = z // 4 == h
    has_below = slab > 0
    has_above = slab < 7

    def copy_to(device, src, dst, send, recv):
        return pltpu.make_async_remote_copy(
            src_ref=src, dst_ref=dst, send_sem=send, recv_sem=recv, device_id=device, device_id_type=MESH
        )

    def owner(j):
        brick, lo, quarter = j // 8, lax.rem(j // 4, 2), lax.rem(j, 4)
        mine = (brick == h) & (lo == x_lo) & (4 * h + quarter == z)
        return brick, lo, quarter, mine, ((4 * h + quarter) * 4 + lo * 2 + core, 2 * slab + brick)

    def giver(j):
        mine = in_half & (j == z * 2 + x_lo)
        return mine, (j * 2 + core, 2 * slab + z // 4)

    mine_rows = pl.ds(pl.multiple_of(h * SHIFT, 8), ROWS)
    pair_rows = pl.ds(pl.multiple_of((1 - h) * SHIFT, 8), ROWS)
    own = pl.ds(2 * h, 2)
    theirs = pl.ds(2 - 2 * h, 2)
    body = pl.ds(PAD, ROWS)

    loads = [
        pltpu.make_async_copy(now_ref.at[0, :, mine_rows], u.at[1, own, body], local_sem.at[0]),
        pltpu.make_async_copy(kappa_ref.at[:, mine_rows], model.at[own], local_sem.at[1]),
        pltpu.make_async_copy(before_ref.at[0, :, mine_rows], u.at[0, own, body], local_sem.at[2]),
        pltpu.make_async_copy(kappa_ref, kappa_rows.at[:, pl.ds(PAD, 512)], local_sem.at[3]),
    ]
    for load in loads:
        load.start()

    barrier = pltpu.get_barrier_semaphore()
    for device in (pair, above, below, other, twin):
        pl.semaphore_signal(barrier, inc=1, device_id=device, device_id_type=MESH)

    def greet(j, carry):
        _, _, _, mine, device = owner(j)

        @pl.when(jnp.logical_not(mine))
        def _():
            pl.semaphore_signal(barrier, inc=1, device_id=device, device_id_type=MESH)

        mine_too, device_too = giver(j)

        @pl.when(jnp.logical_not(mine_too))
        def _():
            pl.semaphore_signal(barrier, inc=1, device_id=device_too, device_id_type=MESH)

        return carry

    lax.fori_loop(0, 16, greet, 0)
    pl.semaphore_wait(barrier, 37 - 2 * in_half.astype(jnp.int32))

    exchange = [
        copy_to(pair, now_ref.at[0, :, pair_rows], u.at[1, own, body], pair_send.at[0], pair_recv.at[0]),
        copy_to(pair, kappa_ref.at[:, pair_rows], model.at[own], pair_send.at[1], pair_recv.at[1]),
        copy_to(pair, before_ref.at[0, :, pair_rows], u.at[0, own, body], pair_send.at[2], pair_recv.at[2]),
    ]
    for copy in exchange:
        copy.start()
    band_rows = pl.ds(pl.multiple_of(shot * 16, 8), 16)
    rims = [
        copy_to(next_dom, kappa_ref.at[1, band_rows], kappa_rim.at[0], rim_send.at[0], rim_recv.at[0]),
        copy_to(last_dom, kappa_ref.at[0, band_rows], kappa_rim.at[1], rim_send.at[1], rim_recv.at[1]),
    ]
    for copy in rims:
        copy.start()

    for n in range(6):
        for p in range(PLANES):
            u[n, p, 0:PAD] = jnp.zeros((PAD, 128), jnp.float32)
            u[n, p, PAD + ROWS : 2 * PAD + ROWS] = jnp.zeros((PAD, 128), jnp.float32)
    for n in range(3):
        for p in range(PLANES):
            weighted[n, p, 0:PAD] = jnp.zeros((PAD, 128), jnp.float32)
            weighted[n, p, PAD + ROWS : 2 * PAD + ROWS] = jnp.zeros((PAD, 128), jnp.float32)
    for p in range(2):
        kappa_rows[p, 0:PAD] = jnp.zeros((PAD, 128), jnp.float32)
        kappa_rows[p, PAD + 512 : 2 * PAD + 512] = jnp.zeros((PAD, 128), jnp.float32)

    cell = receiver_ref[...]
    plane = lax.shift_right_logical(cell, 16) - PLANES * slab
    row = lax.bitwise_and(lax.shift_right_logical(cell, 7), 511) - SHIFT * h
    inside = (plane >= 0) & (plane < PLANES) & (row >= 0) & (row < ROWS)
    cell_row = jnp.where(inside, plane * ROWS + row, -1)
    lane = lax.bitwise_and(cell, 127)

    def fill_rows(i, carry):
        start = pl.multiple_of(i * 16, 16)
        ids = lax.broadcasted_iota(jnp.int32, (16, 2048), 0) + start
        onehot_rows[pl.ds(start, 16)] = jnp.where(ids == cell_row, 1.0, 0.0).astype(jnp.bfloat16)
        return carry

    lax.fori_loop(0, CELL_ROWS // 16, fill_rows, 0)

    values = observed_ref[0]
    high = values.astype(jnp.bfloat16).astype(jnp.float32)
    low = values - high

    def fill_lanes(i, carry):
        start = pl.multiple_of(i * 16, 16)
        hit = lax.broadcasted_iota(jnp.int32, (16, 2048), 0) + start == lane
        onehot_lanes[pl.ds(start, 16)] = jnp.where(hit, 1.0, 0.0).astype(jnp.bfloat16)
        for n in range(NT):
            onehot_lanes[pl.ds(128 * (1 + n) + start, 16)] = jnp.where(hit, high[n : n + 1], 0.0).astype(jnp.bfloat16)
            onehot_lanes[pl.ds(128 * (5 + n) + start, 16)] = jnp.where(hit, low[n : n + 1], 0.0).astype(jnp.bfloat16)
        return carry

    lax.fori_loop(0, 8, fill_lanes, 0)

    def spread(i, carry):
        start = pl.multiple_of(i * TILE, 16)
        product = lax.dot_general(
            onehot_rows[pl.ds(start, TILE)], onehot_lanes[...], (((1,), (1,)), ((), ())),
            preferred_element_type=jnp.float32,
        )
        counts[0, pl.ds(start, TILE)] = product[:, 0:128]
        for n in range(NT):
            counts[1 + n, pl.ds(start, TILE)] = (
                product[:, 128 * (1 + n) : 128 * (2 + n)] + product[:, 128 * (5 + n) : 128 * (6 + n)]
            )
        return carry

    lax.fori_loop(0, CELL_ROWS // TILE, spread, 0)

    spot = source_ref[0]
    spot_plane = lax.shift_right_logical(spot, 16) - PLANES * slab
    spot_row = lax.bitwise_and(lax.shift_right_logical(spot, 7), 511) - SHIFT * h
    spot_lane = lax.bitwise_and(spot, 127)
    lanes = lax.broadcasted_iota(jnp.int32, (BLOCK, 128), 1)
    block_rows = lax.broadcasted_iota(jnp.int32, (BLOCK, 128), 0)
    first_lane = lanes == 0
    last_lane = lanes == 127

    def laplace(field, rim, p, r):
        middle = field[p, pl.ds(PAD + r, BLOCK)]
        if p < PLANES - 1:
            after = field[p + 1, pl.ds(PAD + r, BLOCK)]
        else:
            after = jnp.where(has_above, rim[1, pl.ds(r, BLOCK)], 0.0)
        if p > 0:
            prior = field[p - 1, pl.ds(PAD + r, BLOCK)]
        else:
            prior = jnp.where(has_below, rim[0, pl.ds(r, BLOCK)], 0.0)
        total = after + prior
        total = total + field[p, pl.ds(PAD + 1 + r, BLOCK)] + field[p, pl.ds(PAD - 1 + r, BLOCK)]
        total = total + jnp.where(last_lane, 0.0, pltpu.roll(middle, 127, 1))
        total = total + jnp.where(first_lane, 0.0, pltpu.roll(middle, 1, 1))
        return total - 6.0 * middle, middle

    def forward(n, planes, first, size):
        def block(i, carry):
            r = pl.multiple_of(first + i * BLOCK, 8)
            for p in planes:
                lap, middle = laplace(u.at[n + 1], halo.at[n], p, r)
                speed = model[p, pl.ds(r, BLOCK)]
                pulse = jnp.where(
                    (spot_plane == p) & (spot_lane == lanes) & (spot_row - r == block_rows), wavelet_ref[0, n], 0.0
                )
                after = 2.0 * middle - u[n, p, pl.ds(PAD + r, BLOCK)] + speed * lap + pulse
                u[n + 2, p, pl.ds(PAD + r, BLOCK)] = after
                if n < NT - 1:
                    laps[n, p, pl.ds(r, BLOCK)] = lap
                else:
                    miss = counts[0, pl.ds(p * ROWS + r, BLOCK)] * after - counts[NT, pl.ds(p * ROWS + r, BLOCK)]
                    adjoint[0, p, pl.ds(r, BLOCK)] = miss
                    weighted[0, p, pl.ds(PAD + r, BLOCK)] = speed * miss
                    image[p, pl.ds(r, BLOCK)] = miss * lap
            return carry

        lax.fori_loop(0, size // BLOCK, block, 0)

    def backward(j, planes, first, size):
        level = NT - 1 - j

        def block(i, carry):
            r = pl.multiple_of(first + i * BLOCK, 8)
            for p in planes:
                lap, _ = laplace(weighted.at[j], halo.at[NT + j], p, r)
                at = pl.ds(p * ROWS + r, BLOCK)
                miss = counts[0, at] * u[level + 1, p, pl.ds(PAD + r, BLOCK)] - counts[level, at]
                field = 2.0 * adjoint[j, p, pl.ds(r, BLOCK)] + lap + miss
                if j > 0:
                    field = field - adjoint[j - 1, p, pl.ds(r, BLOCK)]
                image[p, pl.ds(r, BLOCK)] += field * laps[level - 1, p, pl.ds(r, BLOCK)]
                if level > 1:
                    adjoint[j + 1, p, pl.ds(r, BLOCK)] = field
                    weighted[j + 1, p, pl.ds(PAD + r, BLOCK)] = model[p, pl.ds(r, BLOCK)] * field
            return carry

        lax.fori_loop(0, size // BLOCK, block, 0)

    def rim_copies(field, n, c):
        first, size = CHUNKS[c]
        at, to = pl.ds(PAD + first, size), pl.ds(first, size)
        return (
            copy_to(above, field.at[PLANES - 1, at], halo.at[n, 0, to], halo_send.at[n, c, 0], halo_recv.at[n, c, 0]),
            copy_to(below, field.at[0, at], halo.at[n, 1, to], halo_send.at[n, c, 1], halo_recv.at[n, c, 1]),
        )

    halos = []

    def send_rims(field, n, c):
        for copy in rim_copies(field, n, c):
            copy.start()
            halos.append(copy)

    loads[0].wait()
    exchange[0].wait_recv()
    for c in range(len(CHUNKS)):
        send_rims(u.at[1], 0, c)
    for load in loads[1:]:
        load.wait()
    exchange[1].wait_recv()
    exchange[2].wait_recv()

    for n in range(NT):
        forward(n, (1, 2), 0, ROWS)
        for c, (first, size) in enumerate(CHUNKS):
            for copy in rim_copies(u.at[n + 1], n, c):
                copy.wait_recv()
            forward(n, (0, 3), first, size)
            if n < NT - 1:
                send_rims(u.at[n + 2], n + 1, c)
            else:
                send_rims(weighted.at[0], NT, c)

    half = pl.ds(pl.multiple_of(h * 256, 8), 256)
    kept = pl.ds(pl.multiple_of(PAD + 8 * h, 8), 256)
    store = pltpu.make_async_copy(u.at[NT + 1, own, kept], next_ref.at[0, :, half], next_sem.at[0])
    give = copy_to(pair, u.at[NT + 1, theirs, kept], next_ref.at[0, :, half], next_sem.at[1], next_sem.at[2])
    store.start()
    give.start()

    for j in range(NT - 1):
        backward(j, (1, 2), 0, ROWS)
        for c, (first, size) in enumerate(CHUNKS):
            for copy in rim_copies(weighted.at[j], NT + j, c):
                copy.wait_recv()
            backward(j, (0, 3), first, size)
            if j < NT - 2:
                send_rims(weighted.at[j + 1], NT + j + 1, c)

    def band(j, parity):
        return pl.ds(pl.multiple_of(8 * h + 16 * (2 * j + parity), 8), 16)

    def core_copy(j):
        return copy_to(twin, image.at[:, band(j, 1 - core)], mate.at[j], core_send.at[j], core_recv.at[j])

    def core_start(j, carry):
        core_copy(j).start()
        return carry

    def core_sum(j, carry):
        core_copy(j).wait_recv()
        summed[j] = image[:, band(j, core)] + mate[j]
        return carry

    lax.fori_loop(0, 8, core_start, 0)
    lax.fori_loop(0, 8, core_sum, 0)

    slot = z * 2 + x_lo

    def band_copy(j):
        brick, lo, quarter, mine, device = owner(j)
        src = summed.at[quarter * 2 + lo, pl.ds(2 * brick, 2)]
        return mine, copy_to(device, src, landed.at[slot], band_send.at[j], band_recv.at[slot])

    def band_start(j, carry):
        mine, copy = band_copy(j)

        @pl.when(jnp.logical_not(mine))
        def _():
            copy.start()

        return carry

    lax.fori_loop(0, 16, band_start, 0)

    @pl.when(in_half)
    def _():
        landed[slot] = summed[(z - 4 * h) * 2 + x_lo, pl.ds(2 * h, 2)]

    for copy in rims:
        copy.wait_recv()

    band_lanes = lax.broadcasted_iota(jnp.int32, (16, 128), 1)
    start = pl.multiple_of(PAD + shot * 16, 8)
    for p in range(2):
        middle = kappa_rows[p, pl.ds(start, 16)]
        if p == 0:
            after = kappa_rows[1, pl.ds(start, 16)]
            prior = jnp.where(dom > 0, kappa_rim[0], 0.0)
        else:
            after = jnp.where(dom < 15, kappa_rim[1], 0.0)
            prior = kappa_rows[0, pl.ds(start, 16)]
        total = after + prior
        total = total + kappa_rows[p, pl.ds(start + 1, 16)] + kappa_rows[p, pl.ds(start - 1, 16)]
        total = total + jnp.where(band_lanes == 127, 0.0, pltpu.roll(middle, 127, 1))
        total = total + jnp.where(band_lanes == 0, 0.0, pltpu.roll(middle, 1, 1))
        gradient_ref[p] = (total / 6.0 - middle) * PRIOR_GAIN

    def band_wait(j, carry):
        mine, _ = giver(j)

        @pl.when(jnp.logical_not(mine))
        def _():
            copy_to(twin, landed.at[j], landed.at[j], band_send.at[j], band_recv.at[j]).wait_recv()

        return carry

    lax.fori_loop(0, 16, band_wait, 0)
    total = landed[0]
    for j in range(1, 16):
        total = total + landed[j]
    gradient_ref[...] = total / NT - gradient_ref[...]

    def band_done(j, carry):
        mine, copy = band_copy(j)

        @pl.when(jnp.logical_not(mine))
        def _():
            copy.wait_send()

        return carry

    def core_done(j, carry):
        core_copy(j).wait_send()
        return carry

    store.wait()
    give.wait()
    for copy in exchange + rims + halos:
        copy.wait_send()
    lax.fori_loop(0, 8, core_done, 0)
    lax.fori_loop(0, 16, band_done, 0)


def shards(kappa, wave_now, wave_before, wavelet, source_cell, receiver_cells, observed):
    f32 = jnp.float32
    chunks = len(CHUNKS)
    anywhere = pl.BlockSpec(memory_space=pl.ANY)
    vmem = pl.BlockSpec(memory_space=pltpu.VMEM)
    smem = pl.BlockSpec(memory_space=pltpu.SMEM)
    dma = pltpu.SemaphoreType.DMA
    return pl.pallas_call(
        kernel,
        out_shape=(
            jax.ShapeDtypeStruct((2, 16, 128), f32),
            jax.ShapeDtypeStruct(wave_now.shape, f32),
        ),
        in_specs=[anywhere, anywhere, anywhere, smem, smem, vmem, vmem],
        out_specs=(vmem, anywhere),
        scratch_shapes=[
            pltpu.VMEM((6, PLANES, ROWS + 2 * PAD, 128), f32),
            pltpu.VMEM((PLANES, ROWS, 128), f32),
            pltpu.VMEM((8, 128), f32),
            pltpu.VMEM((3, PLANES, ROWS, 128), f32),
            pltpu.VMEM((5, CELL_ROWS, 128), f32),
            pltpu.VMEM((3, PLANES, ROWS, 128), f32),
            pltpu.VMEM((3, PLANES, ROWS + 2 * PAD, 128), f32),
            pltpu.VMEM((7, 2, ROWS, 128), f32),
            pltpu.VMEM((PLANES, ROWS, 128), f32),
            pltpu.VMEM((CELL_ROWS, 2048), jnp.bfloat16),
            pltpu.VMEM((COLUMNS, 2048), jnp.bfloat16),
            pltpu.VMEM((2, 512 + 2 * PAD, 128), f32),
            pltpu.VMEM((2, 16, 128), f32),
            pltpu.VMEM((8, PLANES, 16, 128), f32),
            pltpu.VMEM((8, PLANES, 16, 128), f32),
            pltpu.VMEM((16, 2, 16, 128), f32),
            dma((4,)),
            dma((3,)),
            dma((3,)),
            dma((2,)),
            dma((2,)),
            dma((7, chunks, 2)),
            dma((7, chunks, 2)),
            dma((3,)),
            dma((8,)),
            dma((8,)),
            dma((16,)),
            dma((16,)),
        ],
        name="window",
        compiler_params=pltpu.CompilerParams(
            collective_id=0, has_side_effects=True, vmem_limit_bytes=56 << 20
        ),
    )(kappa, wave_now, wave_before, wavelet, source_cell, receiver_cells, observed)


def solution(mesh):
    return jax.shard_map(
        shards,
        mesh=mesh,
        in_specs=(
            P("dom", None, None),
            P("shot", "dom", None, None),
            P("shot", "dom", None, None),
            P("shot", None),
            P("shot"),
            P("shot", None),
            P("shot", None, None),
        ),
        out_specs=(P("dom", "shot", None), P("shot", "dom", None, None)),
        check_vma=False,
    )
```

```python
import jax
import jax.numpy as jnp
from jax import lax
from jax.experimental import pallas as pl
from jax.experimental.pallas import tpu as pltpu
from jax.sharding import PartitionSpec as P


NT = 4
PRIOR_GAIN = 50.0
PLANES = 4
ROWS = 264
SHIFT = 248
PAD = 8
BLOCK = 24
CHUNKS = ((0, 48), (48, 48), (96, 48), (144, 48), (192, 48), (240, 24))
INNER = (1, 2)
OUTER = (0, 3)
CELL_ROWS = PLANES * ROWS
TILE = 352
COLUMNS = 9 * 128
MESH = pl.DeviceIdType.MESH


def kernel(
    kappa_ref, now_ref, before_ref, wavelet_ref, source_ref, receiver_ref, observed_ref,
    gradient_ref, next_ref,
    u, model, laps, counts, adjoint, weighted, halo, image, cells, values_seen,
    onehot_rows, onehot_lanes, kappa_rows, kappa_rim, mate, shared, crossed, gathered, landed,
    local_sem, pair_send, pair_recv, rim_send, rim_recv, halo_send, halo_recv,
    next_sem, core_send, core_recv, ring_send, ring_recv, band_send, band_recv,
):
    shot = lax.axis_index("shot")
    dom = lax.axis_index("dom")
    h = lax.rem(dom, 2)
    slab = dom // 2
    core = lax.rem(shot, 2)
    x_lo = lax.rem(shot // 2, 2)
    z = shot // 4
    pair = (shot, dom + 1 - 2 * h)
    above = (shot, lax.rem(dom + 2, 16))
    below = (shot, lax.rem(dom + 14, 16))
    next_dom = (shot, lax.rem(dom + 1, 16))
    last_dom = (shot, lax.rem(dom + 15, 16))
    other = (shot, lax.rem(dom + 15 + 2 * h, 16))
    twin = (shot + 1 - 2 * core, dom)
    x = 2 * h + x_lo
    has_below = slab > 0
    has_above = slab < 7

    def copy_to(device, src, dst, send, recv):
        return pltpu.make_async_remote_copy(
            src_ref=src, dst_ref=dst, send_sem=send, recv_sem=recv, device_id=device, device_id_type=MESH
        )

    def ring_device(k):
        at = lax.rem(x + k, 4)
        return at, (z * 4 + lax.rem(at, 2) * 2 + core, 2 * slab + at // 2)

    def stack_device(k):
        at = lax.rem(z + k, 8)
        return at, (at * 4 + x_lo * 2 + core, dom)

    mine_rows = pl.ds(pl.multiple_of(h * SHIFT, 8), ROWS)
    pair_rows = pl.ds(pl.multiple_of((1 - h) * SHIFT, 8), ROWS)
    own = pl.ds(2 * h, 2)
    theirs = pl.ds(2 - 2 * h, 2)
    body = pl.ds(PAD, ROWS)

    barrier = pltpu.get_barrier_semaphore()
    greeted = [pair, above, below, other, twin, ring_device(1)[1], ring_device(3)[1]]
    greeted += [stack_device(k)[1] for k in range(1, 8)]
    for device in greeted:
        pl.semaphore_signal(barrier, inc=1, device_id=device, device_id_type=MESH)

    loads = [
        pltpu.make_async_copy(receiver_ref, cells, local_sem.at[4]),
        pltpu.make_async_copy(observed_ref, values_seen, local_sem.at[5]),
        pltpu.make_async_copy(now_ref.at[0, :, mine_rows], u.at[1, own, body], local_sem.at[0]),
        pltpu.make_async_copy(kappa_ref.at[:, mine_rows], model.at[own], local_sem.at[1]),
        pltpu.make_async_copy(before_ref.at[0, :, mine_rows], u.at[0, own, body], local_sem.at[2]),
        pltpu.make_async_copy(kappa_ref, kappa_rows.at[:, pl.ds(PAD, 512)], local_sem.at[3]),
    ]
    for load in loads:
        load.start()
    pl.semaphore_wait(barrier, len(greeted))

    exchange = [
        copy_to(pair, now_ref.at[0, :, pair_rows], u.at[1, own, body], pair_send.at[0], pair_recv.at[0]),
        copy_to(pair, kappa_ref.at[:, pair_rows], model.at[own], pair_send.at[1], pair_recv.at[1]),
        copy_to(pair, before_ref.at[0, :, pair_rows], u.at[0, own, body], pair_send.at[2], pair_recv.at[2]),
    ]
    for copy in exchange:
        copy.start()
    band_rows = pl.ds(pl.multiple_of(shot * 16, 8), 16)
    rims = [
        copy_to(next_dom, kappa_ref.at[1, band_rows], kappa_rim.at[0], rim_send.at[0], rim_recv.at[0]),
        copy_to(last_dom, kappa_ref.at[0, band_rows], kappa_rim.at[1], rim_send.at[1], rim_recv.at[1]),
    ]
    for copy in rims:
        copy.start()

    for n in range(6):
        for p in range(PLANES):
            u[n, p, 0:PAD] = jnp.zeros((PAD, 128), jnp.float32)
            u[n, p, PAD + ROWS : 2 * PAD + ROWS] = jnp.zeros((PAD, 128), jnp.float32)
    for n in range(3):
        for p in range(PLANES):
            weighted[n, p, 0:PAD] = jnp.zeros((PAD, 128), jnp.float32)
            weighted[n, p, PAD + ROWS : 2 * PAD + ROWS] = jnp.zeros((PAD, 128), jnp.float32)
    for p in range(2):
        kappa_rows[p, 0:PAD] = jnp.zeros((PAD, 128), jnp.float32)
        kappa_rows[p, PAD + 512 : 2 * PAD + 512] = jnp.zeros((PAD, 128), jnp.float32)

    loads[0].wait()
    loads[1].wait()
    cell = cells[...]
    plane = lax.shift_right_logical(cell, 16) - PLANES * slab
    row = lax.bitwise_and(lax.shift_right_logical(cell, 7), 511) - SHIFT * h
    inside = (plane >= 0) & (plane < PLANES) & (row >= 0) & (row < ROWS)
    cell_row = jnp.where(inside, plane * ROWS + row, -1)
    lane = lax.bitwise_and(cell, 127)

    def fill_rows(i, carry):
        start = pl.multiple_of(i * 16, 16)
        ids = lax.broadcasted_iota(jnp.int32, (16, 2048), 0) + start
        onehot_rows[pl.ds(start, 16)] = jnp.where(ids == cell_row, 1.0, 0.0).astype(jnp.bfloat16)
        return carry

    lax.fori_loop(0, CELL_ROWS // 16, fill_rows, 0)

    values = values_seen[0]
    high = values.astype(jnp.bfloat16).astype(jnp.float32)
    low = values - high

    def fill_lanes(i, carry):
        start = pl.multiple_of(i * 16, 16)
        hit = lax.broadcasted_iota(jnp.int32, (16, 2048), 0) + start == lane
        onehot_lanes[pl.ds(start, 16)] = jnp.where(hit, 1.0, 0.0).astype(jnp.bfloat16)
        for n in range(NT):
            onehot_lanes[pl.ds(128 * (1 + n) + start, 16)] = jnp.where(hit, high[n : n + 1], 0.0).astype(jnp.bfloat16)
            onehot_lanes[pl.ds(128 * (5 + n) + start, 16)] = jnp.where(hit, low[n : n + 1], 0.0).astype(jnp.bfloat16)
        return carry

    lax.fori_loop(0, 8, fill_lanes, 0)

    def spread(i, carry):
        start = pl.multiple_of(i * TILE, 16)
        product = lax.dot_general(
            onehot_rows[pl.ds(start, TILE)], onehot_lanes[...], (((1,), (1,)), ((), ())),
            preferred_element_type=jnp.float32,
        )
        counts[0, pl.ds(start, TILE)] = product[:, 0:128]
        for n in range(NT):
            counts[1 + n, pl.ds(start, TILE)] = (
                product[:, 128 * (1 + n) : 128 * (2 + n)] + product[:, 128 * (5 + n) : 128 * (6 + n)]
            )
        return carry

    lax.fori_loop(0, CELL_ROWS // TILE, spread, 0)

    spot = source_ref[0]
    spot_plane = lax.shift_right_logical(spot, 16) - PLANES * slab
    spot_row = lax.bitwise_and(lax.shift_right_logical(spot, 7), 511) - SHIFT * h
    spot_lane = lax.bitwise_and(spot, 127)
    lanes = lax.broadcasted_iota(jnp.int32, (BLOCK, 128), 1)
    block_rows = lax.broadcasted_iota(jnp.int32, (BLOCK, 128), 0)
    first_lane = lanes == 0
    last_lane = lanes == 127

    def laplace(field, rim, p, r):
        middle = field[p, pl.ds(PAD + r, BLOCK)]
        if p < PLANES - 1:
            after = field[p + 1, pl.ds(PAD + r, BLOCK)]
        else:
            after = jnp.where(has_above, rim[1, pl.ds(r, BLOCK)], 0.0)
        if p > 0:
            prior = field[p - 1, pl.ds(PAD + r, BLOCK)]
        else:
            prior = jnp.where(has_below, rim[0, pl.ds(r, BLOCK)], 0.0)
        total = after + prior
        total = total + field[p, pl.ds(PAD + 1 + r, BLOCK)] + field[p, pl.ds(PAD - 1 + r, BLOCK)]
        total = total + jnp.where(last_lane, 0.0, pltpu.roll(middle, 127, 1))
        total = total + jnp.where(first_lane, 0.0, pltpu.roll(middle, 1, 1))
        return total - 6.0 * middle, middle

    def forward(n, planes, first, size):
        def block(i, carry):
            r = pl.multiple_of(first + i * BLOCK, 8)
            for p in planes:
                lap, middle = laplace(u.at[n + 1], halo.at[n], p, r)
                speed = model[p, pl.ds(r, BLOCK)]
                pulse = jnp.where(
                    (spot_plane == p) & (spot_lane == lanes) & (spot_row - r == block_rows), wavelet_ref[0, n], 0.0
                )
                after = 2.0 * middle - u[n, p, pl.ds(PAD + r, BLOCK)] + speed * lap + pulse
                u[n + 2, p, pl.ds(PAD + r, BLOCK)] = after
                if n < NT - 1:
                    laps[n, p, pl.ds(r, BLOCK)] = lap
                else:
                    miss = counts[0, pl.ds(p * ROWS + r, BLOCK)] * after - counts[NT, pl.ds(p * ROWS + r, BLOCK)]
                    adjoint[0, p, pl.ds(r, BLOCK)] = miss
                    weighted[0, p, pl.ds(PAD + r, BLOCK)] = speed * miss
                    image[int(p in OUTER), p // 2, pl.ds(r, BLOCK)] = miss * lap
            return carry

        lax.fori_loop(0, size // BLOCK, block, 0)

    def backward(j, planes, first, size):
        level = NT - 1 - j

        def block(i, carry):
            r = pl.multiple_of(first + i * BLOCK, 8)
            for p in planes:
                lap, _ = laplace(weighted.at[j], halo.at[NT + j], p, r)
                at = pl.ds(p * ROWS + r, BLOCK)
                miss = counts[0, at] * u[level + 1, p, pl.ds(PAD + r, BLOCK)] - counts[level, at]
                field = 2.0 * adjoint[j, p, pl.ds(r, BLOCK)] + lap + miss
                if j > 0:
                    field = field - adjoint[j - 1, p, pl.ds(r, BLOCK)]
                image[int(p in OUTER), p // 2, pl.ds(r, BLOCK)] += field * laps[level - 1, p, pl.ds(r, BLOCK)]
                if level > 1:
                    adjoint[j + 1, p, pl.ds(r, BLOCK)] = field
                    weighted[j + 1, p, pl.ds(PAD + r, BLOCK)] = model[p, pl.ds(r, BLOCK)] * field
            return carry

        lax.fori_loop(0, size // BLOCK, block, 0)

    def rim_copies(field, n, c):
        first, size = CHUNKS[c]
        at, to = pl.ds(PAD + first, size), pl.ds(first, size)
        return (
            copy_to(above, field.at[PLANES - 1, at], halo.at[n, 0, to], halo_send.at[n, c, 0], halo_recv.at[n, c, 0]),
            copy_to(below, field.at[0, at], halo.at[n, 1, to], halo_send.at[n, c, 1], halo_recv.at[n, c, 1]),
        )

    halos = []

    def send_rims(field, n, c):
        for copy in rim_copies(field, n, c):
            copy.start()
            halos.append(copy)

    loads[2].wait()
    exchange[0].wait_recv()
    for c in range(len(CHUNKS)):
        send_rims(u.at[1], 0, c)
    for load in loads[3:]:
        load.wait()
    exchange[1].wait_recv()
    exchange[2].wait_recv()

    for n in range(NT):
        forward(n, INNER, 0, ROWS)
        for c, (first, size) in enumerate(CHUNKS):
            for copy in rim_copies(u.at[n + 1], n, c):
                copy.wait_recv()
            forward(n, OUTER, first, size)
            if n < NT - 1:
                send_rims(u.at[n + 2], n + 1, c)
            else:
                send_rims(weighted.at[0], NT, c)

    half = pl.ds(pl.multiple_of(h * 256, 8), 256)
    kept = pl.ds(pl.multiple_of(PAD + 8 * h, 8), 256)
    store = pltpu.make_async_copy(u.at[NT + 1, own, kept], next_ref.at[0, :, half], next_sem.at[0])
    give = copy_to(pair, u.at[NT + 1, theirs, kept], next_ref.at[0, :, half], next_sem.at[1], next_sem.at[2])
    store.start()
    give.start()

    def band(j, parity):
        return pl.ds(pl.multiple_of(8 * h + 16 * (2 * j + parity), 8), 16)

    def core_copy(part, j):
        return copy_to(
            twin, image.at[part, :, band(j, 1 - core)], mate.at[part, j], core_send.at[part, j], core_recv.at[part, j]
        )

    def core_start(part):
        def step(j, carry):
            core_copy(part, j).start()
            return carry

        lax.fori_loop(0, 8, step, 0)

    def ring_copy(part, k):
        at, device = ring_device(k)
        src = shared.at[part, at // 2, lax.rem(at, 2)]
        return copy_to(device, src, crossed.at[part, x], ring_send.at[part, k], ring_recv.at[part, x])

    def core_finish(part):
        def step(j, carry):
            core_copy(part, j).wait_recv()
            shared[part, :, lax.rem(j, 2), j // 2] = image[part, :, band(j, core)] + mate[part, j]
            return carry

        lax.fori_loop(0, 8, step, 0)
        for k in range(1, 4):
            ring_copy(part, k).start()
        crossed[part, x] = shared[part, h, x_lo]

    def stack_copy(part, k):
        at, device = stack_device(k)
        return copy_to(device, gathered.at[part, at], landed.at[part, z], band_send.at[part, k], band_recv.at[part, z])

    def ring_finish(part):
        for k in range(1, 4):
            at, _ = ring_device(k)
            copy_to(twin, crossed.at[part, at], crossed.at[part, at], ring_send.at[part, k], ring_recv.at[part, at]).wait_recv()

        def step(j, carry):
            gathered[part, j] = crossed[part, 0, j] + crossed[part, 1, j]
            gathered[part, 4 + j] = crossed[part, 2, j] + crossed[part, 3, j]
            return carry

        lax.fori_loop(0, 4, step, 0)
        for k in range(1, 8):
            stack_copy(part, k).start()
        landed[part, z] = gathered[part, z]

    def stack_finish(part):
        for k in range(1, 8):
            at, _ = stack_device(k)
            copy_to(twin, landed.at[part, at], landed.at[part, at], band_send.at[part, k], band_recv.at[part, at]).wait_recv()
        total = landed[part, 0]
        for j in range(1, 8):
            total = total + landed[part, j]
        plane_at = h if part else 1 - h
        gradient_ref[plane_at] = total / NT - gradient_ref[plane_at]

    for j in range(NT - 1):
        backward(j, INNER, 0, ROWS)
        if j == NT - 2:
            core_start(0)
            core_finish(0)
        for c, (first, size) in enumerate(CHUNKS):
            for copy in rim_copies(weighted.at[j], NT + j, c):
                copy.wait_recv()
            backward(j, OUTER, first, size)
            if j < NT - 2:
                send_rims(weighted.at[j + 1], NT + j + 1, c)
    core_start(1)
    ring_finish(0)
    core_finish(1)

    for copy in rims:
        copy.wait_recv()

    band_lanes = lax.broadcasted_iota(jnp.int32, (16, 128), 1)
    start = pl.multiple_of(PAD + shot * 16, 8)
    for p in range(2):
        middle = kappa_rows[p, pl.ds(start, 16)]
        if p == 0:
            after = kappa_rows[1, pl.ds(start, 16)]
            prior = jnp.where(dom > 0, kappa_rim[0], 0.0)
        else:
            after = jnp.where(dom < 15, kappa_rim[1], 0.0)
            prior = kappa_rows[0, pl.ds(start, 16)]
        total = after + prior
        total = total + kappa_rows[p, pl.ds(start + 1, 16)] + kappa_rows[p, pl.ds(start - 1, 16)]
        total = total + jnp.where(band_lanes == 127, 0.0, pltpu.roll(middle, 127, 1))
        total = total + jnp.where(band_lanes == 0, 0.0, pltpu.roll(middle, 1, 1))
        gradient_ref[p] = (total / 6.0 - middle) * PRIOR_GAIN

    ring_finish(1)
    stack_finish(0)
    stack_finish(1)

    for part in range(2):
        def step(j, carry):
            core_copy(part, j).wait_send()
            return carry

        lax.fori_loop(0, 8, step, 0)
        for k in range(1, 4):
            ring_copy(part, k).wait_send()
        for k in range(1, 8):
            stack_copy(part, k).wait_send()
    store.wait()
    give.wait()
    for copy in exchange + rims + halos:
        copy.wait_send()


def shards(kappa, wave_now, wave_before, wavelet, source_cell, receiver_cells, observed):
    f32 = jnp.float32
    chunks = len(CHUNKS)
    anywhere = pl.BlockSpec(memory_space=pl.ANY)
    vmem = pl.BlockSpec(memory_space=pltpu.VMEM)
    smem = pl.BlockSpec(memory_space=pltpu.SMEM)
    dma = pltpu.SemaphoreType.DMA
    return pl.pallas_call(
        kernel,
        out_shape=(
            jax.ShapeDtypeStruct((2, 16, 128), f32),
            jax.ShapeDtypeStruct(wave_now.shape, f32),
        ),
        in_specs=[anywhere, anywhere, anywhere, smem, smem, anywhere, anywhere],
        out_specs=(vmem, anywhere),
        scratch_shapes=[
            pltpu.VMEM((6, PLANES, ROWS + 2 * PAD, 128), f32),
            pltpu.VMEM((PLANES, ROWS, 128), f32),
            pltpu.VMEM((3, PLANES, ROWS, 128), f32),
            pltpu.VMEM((5, CELL_ROWS, 128), f32),
            pltpu.VMEM((3, PLANES, ROWS, 128), f32),
            pltpu.VMEM((3, PLANES, ROWS + 2 * PAD, 128), f32),
            pltpu.VMEM((7, 2, ROWS, 128), f32),
            pltpu.VMEM((2, 2, ROWS, 128), f32),
            pltpu.VMEM((1, 2048), jnp.int32),
            pltpu.VMEM((1, NT, 2048), f32),
            pltpu.VMEM((CELL_ROWS, 2048), jnp.bfloat16),
            pltpu.VMEM((COLUMNS, 2048), jnp.bfloat16),
            pltpu.VMEM((2, 512 + 2 * PAD, 128), f32),
            pltpu.VMEM((2, 16, 128), f32),
            pltpu.VMEM((2, 8, 2, 16, 128), f32),
            pltpu.VMEM((2, 2, 2, 4, 16, 128), f32),
            pltpu.VMEM((2, 4, 4, 16, 128), f32),
            pltpu.VMEM((2, 8, 16, 128), f32),
            pltpu.VMEM((2, 8, 16, 128), f32),
            dma((6,)),
            dma((3,)),
            dma((3,)),
            dma((2,)),
            dma((2,)),
            dma((7, chunks, 2)),
            dma((7, chunks, 2)),
            dma((3,)),
            dma((2, 8)),
            dma((2, 8)),
            dma((2, 4)),
            dma((2, 4)),
            dma((2, 8)),
            dma((2, 8)),
        ],
        name="window",
        compiler_params=pltpu.CompilerParams(
            collective_id=0, has_side_effects=True, vmem_limit_bytes=56 << 20
        ),
    )(kappa, wave_now, wave_before, wavelet, source_cell, receiver_cells, observed)


def solution(mesh):
    return jax.shard_map(
        shards,
        mesh=mesh,
        in_specs=(
            P("dom", None, None),
            P("shot", "dom", None, None),
            P("shot", "dom", None, None),
            P("shot", None),
            P("shot"),
            P("shot", None),
            P("shot", None, None),
        ),
        out_specs=(P("dom", "shot", None), P("shot", "dom", None, None)),
        check_vma=False,
    )
```

```python
import jax
import jax.numpy as jnp
from jax import lax
from jax.experimental import pallas as pl
from jax.experimental.pallas import tpu as pltpu
from jax.sharding import PartitionSpec as P


NT = 4
PRIOR_GAIN = 50.0
PLANES = 4
ROWS = 264
SHIFT = 248
PAD = 8
BLOCK = 24
CHUNKS = ((0, 48), (48, 48), (96, 48), (144, 48), (192, 48), (240, 24))
INNER = (1, 2)
OUTER = (0, 3)
CELL_ROWS = PLANES * ROWS
TILE = 352
COLUMNS = 9 * 128
PIECES = 2
MESH = pl.DeviceIdType.MESH


def kernel(
    kappa_ref, now_ref, before_ref, wavelet_ref, source_ref, receiver_ref, observed_ref,
    gradient_ref, next_ref,
    u, model, laps, counts, adjoint, weighted, halo, image, cells, values_seen,
    onehot_rows, onehot_lanes, kappa_rows, kappa_rim, mate, shared, crossed, gathered, landed,
    local_sem, pair_send, pair_recv, share_send, share_recv, rim_send, rim_recv, halo_send, halo_recv,
    next_sem, core_send, core_recv, ring_send, ring_recv, band_send, band_recv,
):
    shot = lax.axis_index("shot")
    dom = lax.axis_index("dom")
    h = lax.rem(dom, 2)
    slab = dom // 2
    core = lax.rem(shot, 2)
    x_lo = lax.rem(shot // 2, 2)
    z = shot // 4
    pair = (shot, dom + 1 - 2 * h)
    above = (shot, lax.rem(dom + 2, 16))
    below = (shot, lax.rem(dom + 14, 16))
    next_dom = (shot, lax.rem(dom + 1, 16))
    last_dom = (shot, lax.rem(dom + 15, 16))
    other = (shot, lax.rem(dom + 15 + 2 * h, 16))
    twin = (shot + 1 - 2 * core, dom)
    x = 2 * h + x_lo
    has_below = slab > 0
    has_above = slab < 7

    def copy_to(device, src, dst, send, recv):
        return pltpu.make_async_remote_copy(
            src_ref=src, dst_ref=dst, send_sem=send, recv_sem=recv, device_id=device, device_id_type=MESH
        )

    def ring_device(k):
        at = lax.rem(x + k, 4)
        return at, (z * 4 + lax.rem(at, 2) * 2 + core, 2 * slab + at // 2)

    def stack_device(k):
        at = lax.rem(z + k, 8)
        return at, (at * 4 + x_lo * 2 + core, dom)

    mine_rows = pl.ds(pl.multiple_of(h * SHIFT, 8), ROWS)
    pair_rows = pl.ds(pl.multiple_of((1 - h) * SHIFT, 8), ROWS)
    own = pl.ds(2 * h, 2)
    theirs = pl.ds(2 - 2 * h, 2)
    body = pl.ds(PAD, ROWS)

    barrier = pltpu.get_barrier_semaphore()
    greeted = [pair, above, below, other, twin, ring_device(1)[1], ring_device(3)[1]]
    greeted += [stack_device(k)[1] for k in range(1, 8)]
    for device in greeted:
        pl.semaphore_signal(barrier, inc=1, device_id=device, device_id_type=MESH)

    loads = [
        pltpu.make_async_copy(receiver_ref, cells, local_sem.at[4]),
        pltpu.make_async_copy(observed_ref, values_seen, local_sem.at[5]),
        pltpu.make_async_copy(now_ref.at[0, :, mine_rows], u.at[1, own, body], local_sem.at[0]),
        pltpu.make_async_copy(kappa_ref.at[:, mine_rows], model.at[own], local_sem.at[1]),
        pltpu.make_async_copy(before_ref.at[0, :, mine_rows], u.at[0, own, body], local_sem.at[2]),
        pltpu.make_async_copy(kappa_ref, kappa_rows.at[:, pl.ds(PAD, 512)], local_sem.at[3]),
    ]
    for load in loads:
        load.start()
    pl.semaphore_wait(barrier, len(greeted))

    def share(first, size):
        return pl.ds(pl.multiple_of(first, 8), size)

    eighth = share(z * 32, 32)
    exchange = [
        copy_to(
            pair, kappa_ref.at[:, share((1 - h) * SHIFT + z * 32, 32)], model.at[own, eighth], pair_send.at[1], pair_recv.at[1]
        ),
        copy_to(
            pair, kappa_ref.at[:, share((1 - h) * SHIFT + 256, 8)], model.at[own, 256:264], pair_send.at[3], pair_recv.at[3]
        ),
        copy_to(pair, now_ref.at[0, :, pair_rows], u.at[1, own, body], pair_send.at[0], pair_recv.at[0]),
        copy_to(pair, before_ref.at[0, :, pair_rows], u.at[0, own, body], pair_send.at[2], pair_recv.at[2]),
    ]
    for copy in exchange:
        copy.start()
    band_rows = pl.ds(pl.multiple_of(shot * 16, 8), 16)
    rims = [
        copy_to(next_dom, kappa_ref.at[1, band_rows], kappa_rim.at[0], rim_send.at[0], rim_recv.at[0]),
        copy_to(last_dom, kappa_ref.at[0, band_rows], kappa_rim.at[1], rim_send.at[1], rim_recv.at[1]),
    ]
    for copy in rims:
        copy.start()

    for n in range(6):
        for p in range(PLANES):
            u[n, p, 0:PAD] = jnp.zeros((PAD, 128), jnp.float32)
            u[n, p, PAD + ROWS : 2 * PAD + ROWS] = jnp.zeros((PAD, 128), jnp.float32)
    for n in range(3):
        for p in range(PLANES):
            weighted[n, p, 0:PAD] = jnp.zeros((PAD, 128), jnp.float32)
            weighted[n, p, PAD + ROWS : 2 * PAD + ROWS] = jnp.zeros((PAD, 128), jnp.float32)
    for p in range(2):
        kappa_rows[p, 0:PAD] = jnp.zeros((PAD, 128), jnp.float32)
        kappa_rows[p, PAD + 512 : 2 * PAD + 512] = jnp.zeros((PAD, 128), jnp.float32)

    loads[0].wait()
    loads[1].wait()
    cell = cells[...]
    plane = lax.shift_right_logical(cell, 16) - PLANES * slab
    row = lax.bitwise_and(lax.shift_right_logical(cell, 7), 511) - SHIFT * h
    inside = (plane >= 0) & (plane < PLANES) & (row >= 0) & (row < ROWS)
    cell_row = jnp.where(inside, plane * ROWS + row, -1)
    lane = lax.bitwise_and(cell, 127)

    def fill_rows(i, carry):
        start = pl.multiple_of(i * 16, 16)
        ids = lax.broadcasted_iota(jnp.int32, (16, 2048), 0) + start
        onehot_rows[pl.ds(start, 16)] = jnp.where(ids == cell_row, 1.0, 0.0).astype(jnp.bfloat16)
        return carry

    lax.fori_loop(0, CELL_ROWS // 16, fill_rows, 0)

    exchange[0].wait_recv()
    passed = []
    for k in range(1, 8):
        part = model.at[theirs, eighth]
        passed.append(copy_to(stack_device(k)[1], part, part, share_send.at[k], share_recv.at[z]))
    for copy in passed:
        copy.start()

    values = values_seen[0]
    high = values.astype(jnp.bfloat16).astype(jnp.float32)
    low = values - high

    def fill_lanes(i, carry):
        start = pl.multiple_of(i * 16, 16)
        hit = lax.broadcasted_iota(jnp.int32, (16, 2048), 0) + start == lane
        onehot_lanes[pl.ds(start, 16)] = jnp.where(hit, 1.0, 0.0).astype(jnp.bfloat16)
        for n in range(NT):
            onehot_lanes[pl.ds(128 * (1 + n) + start, 16)] = jnp.where(hit, high[n : n + 1], 0.0).astype(jnp.bfloat16)
            onehot_lanes[pl.ds(128 * (5 + n) + start, 16)] = jnp.where(hit, low[n : n + 1], 0.0).astype(jnp.bfloat16)
        return carry

    lax.fori_loop(0, 8, fill_lanes, 0)

    def spread(i, carry):
        start = pl.multiple_of(i * TILE, 16)
        product = lax.dot_general(
            onehot_rows[pl.ds(start, TILE)], onehot_lanes[...], (((1,), (1,)), ((), ())),
            preferred_element_type=jnp.float32,
        )
        counts[0, pl.ds(start, TILE)] = product[:, 0:128]
        for n in range(NT):
            counts[1 + n, pl.ds(start, TILE)] = (
                product[:, 128 * (1 + n) : 128 * (2 + n)] + product[:, 128 * (5 + n) : 128 * (6 + n)]
            )
        return carry

    lax.fori_loop(0, CELL_ROWS // TILE, spread, 0)

    spot = source_ref[0]
    spot_plane = lax.shift_right_logical(spot, 16) - PLANES * slab
    spot_row = lax.bitwise_and(lax.shift_right_logical(spot, 7), 511) - SHIFT * h
    spot_lane = lax.bitwise_and(spot, 127)
    lanes = lax.broadcasted_iota(jnp.int32, (BLOCK, 128), 1)
    block_rows = lax.broadcasted_iota(jnp.int32, (BLOCK, 128), 0)
    first_lane = lanes == 0
    last_lane = lanes == 127

    def laplace(field, rim, p, r):
        middle = field[p, pl.ds(PAD + r, BLOCK)]
        if p < PLANES - 1:
            after = field[p + 1, pl.ds(PAD + r, BLOCK)]
        else:
            after = jnp.where(has_above, rim[1, pl.ds(r, BLOCK)], 0.0)
        if p > 0:
            prior = field[p - 1, pl.ds(PAD + r, BLOCK)]
        else:
            prior = jnp.where(has_below, rim[0, pl.ds(r, BLOCK)], 0.0)
        total = after + prior
        total = total + field[p, pl.ds(PAD + 1 + r, BLOCK)] + field[p, pl.ds(PAD - 1 + r, BLOCK)]
        total = total + jnp.where(last_lane, 0.0, pltpu.roll(middle, 127, 1))
        total = total + jnp.where(first_lane, 0.0, pltpu.roll(middle, 1, 1))
        return total - 6.0 * middle, middle

    def forward(n, planes, first, size):
        def block(i, carry):
            r = pl.multiple_of(first + i * BLOCK, 8)
            for p in planes:
                lap, middle = laplace(u.at[n + 1], halo.at[n], p, r)
                speed = model[p, pl.ds(r, BLOCK)]
                pulse = jnp.where(
                    (spot_plane == p) & (spot_lane == lanes) & (spot_row - r == block_rows), wavelet_ref[0, n], 0.0
                )
                after = 2.0 * middle - u[n, p, pl.ds(PAD + r, BLOCK)] + speed * lap + pulse
                u[n + 2, p, pl.ds(PAD + r, BLOCK)] = after
                if n < NT - 1:
                    laps[n, p, pl.ds(r, BLOCK)] = lap
                else:
                    miss = counts[0, pl.ds(p * ROWS + r, BLOCK)] * after - counts[NT, pl.ds(p * ROWS + r, BLOCK)]
                    adjoint[0, p, pl.ds(r, BLOCK)] = miss
                    weighted[0, p, pl.ds(PAD + r, BLOCK)] = speed * miss
                    image[int(p in OUTER), p // 2, pl.ds(r, BLOCK)] = miss * lap
            return carry

        lax.fori_loop(0, size // BLOCK, block, 0)

    def backward(j, planes, first, size):
        level = NT - 1 - j

        def block(i, carry):
            r = pl.multiple_of(first + i * BLOCK, 8)
            for p in planes:
                lap, _ = laplace(weighted.at[j], halo.at[NT + j], p, r)
                at = pl.ds(p * ROWS + r, BLOCK)
                miss = counts[0, at] * u[level + 1, p, pl.ds(PAD + r, BLOCK)] - counts[level, at]
                field = 2.0 * adjoint[j, p, pl.ds(r, BLOCK)] + lap + miss
                if j > 0:
                    field = field - adjoint[j - 1, p, pl.ds(r, BLOCK)]
                image[int(p in OUTER), p // 2, pl.ds(r, BLOCK)] += field * laps[level - 1, p, pl.ds(r, BLOCK)]
                if level > 1:
                    adjoint[j + 1, p, pl.ds(r, BLOCK)] = field
                    weighted[j + 1, p, pl.ds(PAD + r, BLOCK)] = model[p, pl.ds(r, BLOCK)] * field
            return carry

        lax.fori_loop(0, size // BLOCK, block, 0)

    def rim_copies(field, n, c):
        first, size = CHUNKS[c]
        at, to = pl.ds(PAD + first, size), pl.ds(first, size)
        return (
            copy_to(above, field.at[PLANES - 1, at], halo.at[n, 0, to], halo_send.at[n, c, 0], halo_recv.at[n, c, 0]),
            copy_to(below, field.at[0, at], halo.at[n, 1, to], halo_send.at[n, c, 1], halo_recv.at[n, c, 1]),
        )

    halos = []

    def send_rims(field, n, c):
        for copy in rim_copies(field, n, c):
            copy.start()
            halos.append(copy)

    loads[2].wait()
    exchange[2].wait_recv()
    for c in range(len(CHUNKS)):
        send_rims(u.at[1], 0, c)
    for load in loads[3:]:
        load.wait()
    exchange[1].wait_recv()
    for k in range(1, 8):
        at, device = stack_device(k)
        part = model.at[theirs, share(at * 32, 32)]
        copy_to(device, part, part, share_send.at[k], share_recv.at[at]).wait_recv()
    exchange[3].wait_recv()

    for n in range(NT):
        forward(n, INNER, 0, ROWS)
        for c, (first, size) in enumerate(CHUNKS):
            for copy in rim_copies(u.at[n + 1], n, c):
                copy.wait_recv()
            forward(n, OUTER, first, size)
            if n < NT - 1:
                send_rims(u.at[n + 2], n + 1, c)
            else:
                send_rims(weighted.at[0], NT, c)

    half = pl.ds(pl.multiple_of(h * 256, 8), 256)
    kept = pl.ds(pl.multiple_of(PAD + 8 * h, 8), 256)
    store = pltpu.make_async_copy(u.at[NT + 1, own, kept], next_ref.at[0, :, half], next_sem.at[0])
    give = copy_to(pair, u.at[NT + 1, theirs, kept], next_ref.at[0, :, half], next_sem.at[1], next_sem.at[2])
    store.start()
    give.start()

    def band(j, parity):
        return pl.ds(pl.multiple_of(8 * h + 16 * (2 * j + parity), 8), 16)

    def core_copy(part, j):
        return copy_to(
            twin, image.at[part, :, band(j, 1 - core)], mate.at[part, j], core_send.at[part, j], core_recv.at[part, j]
        )

    def core_start(part):
        def step(j, carry):
            core_copy(part, j).start()
            return carry

        lax.fori_loop(0, 8, step, 0)

    def ring_copy(part, k):
        at, device = ring_device(k)
        src = shared.at[part, at // 2, lax.rem(at, 2)]
        return copy_to(device, src, crossed.at[part, x], ring_send.at[part, k], ring_recv.at[part, x])

    def core_finish(part):
        def step(j, carry):
            core_copy(part, j).wait_recv()
            shared[part, :, lax.rem(j, 2), j // 2] = image[part, :, band(j, core)] + mate[part, j]
            return carry

        lax.fori_loop(0, 8, step, 0)
        for k in range(1, 4):
            ring_copy(part, k).start()
        crossed[part, x] = shared[part, h, x_lo]

    def stack_copy(part, k):
        at, device = stack_device(k)
        return copy_to(device, gathered.at[part, at], landed.at[part, z], band_send.at[part, k], band_recv.at[part, z])

    def ring_finish(part):
        for k in range(1, 4):
            at, _ = ring_device(k)
            copy_to(twin, crossed.at[part, at], crossed.at[part, at], ring_send.at[part, k], ring_recv.at[part, at]).wait_recv()

        def step(j, carry):
            gathered[part, j] = crossed[part, 0, j] + crossed[part, 1, j]
            gathered[part, 4 + j] = crossed[part, 2, j] + crossed[part, 3, j]
            return carry

        lax.fori_loop(0, 4, step, 0)
        for k in range(1, 8):
            stack_copy(part, k).start()
        landed[part, z] = gathered[part, z]

    def stack_finish(part):
        for k in range(1, 8):
            at, _ = stack_device(k)
            copy_to(twin, landed.at[part, at], landed.at[part, at], band_send.at[part, k], band_recv.at[part, at]).wait_recv()
        total = landed[part, 0]
        for j in range(1, 8):
            total = total + landed[part, j]
        plane_at = h if part else 1 - h
        gradient_ref[plane_at] = total / NT - gradient_ref[plane_at]

    for j in range(NT - 1):
        backward(j, INNER, 0, ROWS)
        if j == NT - 2:
            core_start(0)
            core_finish(0)
        for c, (first, size) in enumerate(CHUNKS):
            for copy in rim_copies(weighted.at[j], NT + j, c):
                copy.wait_recv()
            backward(j, OUTER, first, size)
            if j < NT - 2:
                send_rims(weighted.at[j + 1], NT + j + 1, c)
    core_start(1)
    ring_finish(0)
    core_finish(1)

    for copy in rims:
        copy.wait_recv()

    band_lanes = lax.broadcasted_iota(jnp.int32, (16, 128), 1)
    start = pl.multiple_of(PAD + shot * 16, 8)
    for p in range(2):
        middle = kappa_rows[p, pl.ds(start, 16)]
        if p == 0:
            after = kappa_rows[1, pl.ds(start, 16)]
            prior = jnp.where(dom > 0, kappa_rim[0], 0.0)
        else:
            after = jnp.where(dom < 15, kappa_rim[1], 0.0)
            prior = kappa_rows[0, pl.ds(start, 16)]
        total = after + prior
        total = total + kappa_rows[p, pl.ds(start + 1, 16)] + kappa_rows[p, pl.ds(start - 1, 16)]
        total = total + jnp.where(band_lanes == 127, 0.0, pltpu.roll(middle, 127, 1))
        total = total + jnp.where(band_lanes == 0, 0.0, pltpu.roll(middle, 1, 1))
        gradient_ref[p] = (total / 6.0 - middle) * PRIOR_GAIN

    ring_finish(1)
    stack_finish(0)
    stack_finish(1)

    for part in range(2):
        def step(j, carry):
            core_copy(part, j).wait_send()
            return carry

        lax.fori_loop(0, 8, step, 0)
        for k in range(1, 4):
            ring_copy(part, k).wait_send()
        for k in range(1, 8):
            stack_copy(part, k).wait_send()
    store.wait()
    give.wait()
    for copy in exchange + passed + rims + halos:
        copy.wait_send()


def hand_over(gradient_ref, next_ref, gradient_out, next_out, gradient, waves, load_sem, store_sem):
    loads, stores = [], []
    for p in range(2):
        for i in range(PIECES):
            rows = pl.ds(i * (512 // PIECES), 512 // PIECES)
            at = 1 + p * PIECES + i
            loads.append(pltpu.make_async_copy(next_ref.at[0, p, rows], waves.at[p, rows], load_sem.at[at]))
            stores.append(pltpu.make_async_copy(waves.at[p, rows], next_out.at[0, p, rows], store_sem.at[at]))
    loads.append(pltpu.make_async_copy(gradient_ref, gradient, load_sem.at[0]))
    stores.append(pltpu.make_async_copy(gradient, gradient_out, store_sem.at[0]))
    for load in loads:
        load.start()
    for load, store in zip(loads, stores):
        load.wait()
        store.start()
    for store in stores:
        store.wait()


def shards(kappa, wave_now, wave_before, wavelet, source_cell, receiver_cells, observed):
    f32 = jnp.float32
    chunks = len(CHUNKS)
    anywhere = pl.BlockSpec(memory_space=pl.ANY)
    vmem = pl.BlockSpec(memory_space=pltpu.VMEM)
    smem = pl.BlockSpec(memory_space=pltpu.SMEM)
    dma = pltpu.SemaphoreType.DMA
    results = pl.pallas_call(
        kernel,
        out_shape=(
            jax.ShapeDtypeStruct((2, 16, 128), f32),
            jax.ShapeDtypeStruct(wave_now.shape, f32),
        ),
        in_specs=[anywhere, anywhere, anywhere, smem, smem, anywhere, anywhere],
        out_specs=(vmem, anywhere),
        scratch_shapes=[
            pltpu.VMEM((6, PLANES, ROWS + 2 * PAD, 128), f32),
            pltpu.VMEM((PLANES, ROWS, 128), f32),
            pltpu.VMEM((3, PLANES, ROWS, 128), f32),
            pltpu.VMEM((5, CELL_ROWS, 128), f32),
            pltpu.VMEM((3, PLANES, ROWS, 128), f32),
            pltpu.VMEM((3, PLANES, ROWS + 2 * PAD, 128), f32),
            pltpu.VMEM((7, 2, ROWS, 128), f32),
            pltpu.VMEM((2, 2, ROWS, 128), f32),
            pltpu.VMEM((1, 2048), jnp.int32),
            pltpu.VMEM((1, NT, 2048), f32),
            pltpu.VMEM((CELL_ROWS, 2048), jnp.bfloat16),
            pltpu.VMEM((COLUMNS, 2048), jnp.bfloat16),
            pltpu.VMEM((2, 512 + 2 * PAD, 128), f32),
            pltpu.VMEM((2, 16, 128), f32),
            pltpu.VMEM((2, 8, 2, 16, 128), f32),
            pltpu.VMEM((2, 2, 2, 4, 16, 128), f32),
            pltpu.VMEM((2, 4, 4, 16, 128), f32),
            pltpu.VMEM((2, 8, 16, 128), f32),
            pltpu.VMEM((2, 8, 16, 128), f32),
            dma((6,)),
            dma((4,)),
            dma((4,)),
            dma((8,)),
            dma((8,)),
            dma((2,)),
            dma((2,)),
            dma((7, chunks, 2)),
            dma((7, chunks, 2)),
            dma((3,)),
            dma((2, 8)),
            dma((2, 8)),
            dma((2, 4)),
            dma((2, 4)),
            dma((2, 8)),
            dma((2, 8)),
        ],
        name="window",
        compiler_params=pltpu.CompilerParams(
            collective_id=0, has_side_effects=True, vmem_limit_bytes=56 << 20
        ),
    )(kappa, wave_now, wave_before, wavelet, source_cell, receiver_cells, observed)
    return pl.pallas_call(
        hand_over,
        out_shape=tuple(jax.ShapeDtypeStruct(r.shape, r.dtype) for r in results),
        in_specs=[anywhere, anywhere],
        out_specs=(anywhere, anywhere),
        scratch_shapes=[
            pltpu.VMEM((2, 16, 128), f32),
            pltpu.VMEM((2, 512, 128), f32),
            dma((1 + 2 * PIECES,)),
            dma((1 + 2 * PIECES,)),
        ],
        name="hand_over",
    )(*results)


def solution(mesh):
    return jax.shard_map(
        shards,
        mesh=mesh,
        in_specs=(
            P("dom", None, None),
            P("shot", "dom", None, None),
            P("shot", "dom", None, None),
            P("shot", None),
            P("shot"),
            P("shot", None),
            P("shot", None, None),
        ),
        out_specs=(P("dom", "shot", None), P("shot", "dom", None, None)),
        check_vma=False,
    )
```

```python
import jax
import jax.numpy as jnp
from jax import lax
from jax.experimental import pallas as pl
from jax.experimental.pallas import tpu as pltpu
from jax.sharding import PartitionSpec as P


NT = 4
PRIOR_GAIN = 50.0
PLANES = 4
ROWS = 264
SHIFT = 248
PAD = 8
BLOCK = 24
CHUNKS = ((0, 48), (48, 48), (96, 48), (144, 48), (192, 48), (240, 24))
HALVES = ((0, 144), (144, 120))
LATER = (2, 2, 3, 3)
INNER = (1, 2)
OUTER = (0, 3)
CELL_ROWS = PLANES * ROWS
TILE = 352
COLUMNS = 9 * 128
PIECES = 2
MESH = pl.DeviceIdType.MESH


def kernel(
    kappa_ref, now_ref, before_ref, wavelet_ref, source_ref, receiver_ref, observed_ref,
    gradient_ref, next_ref,
    u, model, laps, counts, adjoint, weighted, halo, image, cells, values_seen,
    onehot_rows, onehot_lanes, kappa_rows, kappa_rim, mate, shared, crossed, gathered, landed,
    local_sem, pair_send, pair_recv, share_send, share_recv, first_send, first_recv, rim_send, rim_recv, halo_send, halo_recv,
    next_sem, core_send, core_recv, ring_send, ring_recv, band_send, band_recv,
):
    shot = lax.axis_index("shot")
    dom = lax.axis_index("dom")
    h = lax.rem(dom, 2)
    slab = dom // 2
    core = lax.rem(shot, 2)
    x_lo = lax.rem(shot // 2, 2)
    z = shot // 4
    pair = (shot, dom + 1 - 2 * h)
    above = (shot, lax.rem(dom + 2, 16))
    below = (shot, lax.rem(dom + 14, 16))
    next_dom = (shot, lax.rem(dom + 1, 16))
    last_dom = (shot, lax.rem(dom + 15, 16))
    other = (shot, lax.rem(dom + 15 + 2 * h, 16))
    twin = (shot + 1 - 2 * core, dom)
    x = 2 * h + x_lo
    has_below = slab > 0
    has_above = slab < 7

    def copy_to(device, src, dst, send, recv):
        return pltpu.make_async_remote_copy(
            src_ref=src, dst_ref=dst, send_sem=send, recv_sem=recv, device_id=device, device_id_type=MESH
        )

    def ring_device(k):
        at = lax.rem(x + k, 4)
        return at, (z * 4 + lax.rem(at, 2) * 2 + core, 2 * slab + at // 2)

    def stack_device(k):
        at = lax.rem(z + k, 8)
        return at, (at * 4 + x_lo * 2 + core, dom)

    mine_rows = pl.ds(pl.multiple_of(h * SHIFT, 8), ROWS)
    pair_rows = pl.ds(pl.multiple_of((1 - h) * SHIFT, 8), ROWS)
    own = pl.ds(2 * h, 2)
    theirs = pl.ds(2 - 2 * h, 2)
    body = pl.ds(PAD, ROWS)

    barrier = pltpu.get_barrier_semaphore()
    greeted = [pair, above, below, other, twin, ring_device(1)[1], ring_device(3)[1]]
    greeted += [stack_device(k)[1] for k in range(1, 8)]
    for device in greeted:
        pl.semaphore_signal(barrier, inc=1, device_id=device, device_id_type=MESH)

    loads = [
        pltpu.make_async_copy(receiver_ref, cells, local_sem.at[4]),
        pltpu.make_async_copy(observed_ref, values_seen, local_sem.at[5]),
        pltpu.make_async_copy(now_ref.at[0, :, mine_rows], u.at[1, own, body], local_sem.at[0]),
        pltpu.make_async_copy(kappa_ref.at[:, mine_rows], model.at[own], local_sem.at[1]),
        pltpu.make_async_copy(before_ref.at[0, :, mine_rows], u.at[0, own, body], local_sem.at[2]),
        pltpu.make_async_copy(kappa_ref, kappa_rows.at[:, pl.ds(PAD, 512)], local_sem.at[3]),
    ]
    for load in loads:
        load.start()
    for n in range(6):
        for p in range(PLANES):
            u[n, p, 0:PAD] = jnp.zeros((PAD, 128), jnp.float32)
            u[n, p, PAD + ROWS : 2 * PAD + ROWS] = jnp.zeros((PAD, 128), jnp.float32)
    for n in range(3):
        for p in range(PLANES):
            weighted[n, p, 0:PAD] = jnp.zeros((PAD, 128), jnp.float32)
            weighted[n, p, PAD + ROWS : 2 * PAD + ROWS] = jnp.zeros((PAD, 128), jnp.float32)
    for p in range(2):
        kappa_rows[p, 0:PAD] = jnp.zeros((PAD, 128), jnp.float32)
        kappa_rows[p, PAD + 512 : 2 * PAD + 512] = jnp.zeros((PAD, 128), jnp.float32)

    loads[0].wait()
    cell = cells[...]
    plane = lax.shift_right_logical(cell, 16) - PLANES * slab
    row = lax.bitwise_and(lax.shift_right_logical(cell, 7), 511) - SHIFT * h
    inside = (plane >= 0) & (plane < PLANES) & (row >= 0) & (row < ROWS)
    cell_row = jnp.where(inside, plane * ROWS + row, -1)
    lane = lax.bitwise_and(cell, 127)

    def fill_rows(i, carry):
        start = pl.multiple_of(i * 16, 16)
        ids = lax.broadcasted_iota(jnp.int32, (16, 2048), 0) + start
        onehot_rows[pl.ds(start, 16)] = jnp.where(ids == cell_row, 1.0, 0.0).astype(jnp.bfloat16)
        return carry

    lax.fori_loop(0, CELL_ROWS // 16, fill_rows, 0)
    pl.semaphore_wait(barrier, len(greeted))

    def share(first, size):
        return pl.ds(pl.multiple_of(first, 8), size)

    eighth = share(z * 32, 32)

    def outer_copy(i):
        first, size = HALVES[i]
        src = now_ref.at[0, h, share((1 - h) * SHIFT + first, size)]
        return copy_to(pair, src, u.at[1, 3 * h, pl.ds(PAD + first, size)], pair_send.at[4 + i], pair_recv.at[4 + i])

    def relay(i):
        first, size = HALVES[i]
        device = (shot, lax.rem(dom + 2 + 12 * h, 16))
        src = u.at[1, 3 - 3 * h, pl.ds(PAD + first, size)]
        return copy_to(device, src, halo.at[0, h, pl.ds(first, size)], first_send.at[i], first_recv.at[i])

    direct = copy_to(
        (shot, lax.rem(dom + 14 + 4 * h, 16)), now_ref.at[0, h, mine_rows], halo.at[0, 1 - h], first_send.at[2], first_recv.at[2]
    )
    opening = [relay(0), relay(1), direct]

    def kappa_copy(i):
        src = kappa_ref.at[(h, 1 - h)[i], share((1 - h) * SHIFT + z * 32, 32)]
        return copy_to(pair, src, model.at[(3 * h, 1 + h)[i], eighth], pair_send.at[i], pair_recv.at[i])

    def before_copy(i):
        src = before_ref.at[0, (h, 1 - h)[i], pair_rows]
        return copy_to(pair, src, u.at[0, (3 * h, 1 + h)[i], body], pair_send.at[6 + i], pair_recv.at[6 + i])

    exchange = [
        kappa_copy(0),
        copy_to(
            pair, kappa_ref.at[:, share((1 - h) * SHIFT + 256, 8)], model.at[own, 256:264], pair_send.at[2], pair_recv.at[2]
        ),
        outer_copy(0),
        outer_copy(1),
        copy_to(pair, now_ref.at[0, 1 - h, pair_rows], u.at[1, 1 + h, body], pair_send.at[3], pair_recv.at[3]),
        kappa_copy(1),
        before_copy(0),
        before_copy(1),
    ]
    direct.start()
    for copy in exchange:
        copy.start()
    band_rows = pl.ds(pl.multiple_of(shot * 16, 8), 16)
    rims = [
        copy_to(next_dom, kappa_ref.at[1, band_rows], kappa_rim.at[0], rim_send.at[0], rim_recv.at[0]),
        copy_to(last_dom, kappa_ref.at[0, band_rows], kappa_rim.at[1], rim_send.at[1], rim_recv.at[1]),
    ]
    for copy in rims:
        copy.start()

    passed = []

    def pass_on(i):
        part = model.at[(3 - 3 * h, 2 - h)[i], eighth]
        for k in range(1, 8):
            copy = copy_to(stack_device(k)[1], part, part, share_send.at[i, k], share_recv.at[i, z])
            copy.start()
            passed.append(copy)

    def take_over(i):
        for k in range(1, 8):
            at, device = stack_device(k)
            part = model.at[(3 - 3 * h, 2 - h)[i], share(at * 32, 32)]
            copy_to(device, part, part, share_send.at[i, k], share_recv.at[i, at]).wait_recv()

    exchange[0].wait_recv()
    pass_on(0)

    loads[1].wait()
    values = values_seen[0]
    high = values.astype(jnp.bfloat16).astype(jnp.float32)
    low = values - high

    def fill_lanes(i, carry):
        start = pl.multiple_of(i * 16, 16)
        hit = lax.broadcasted_iota(jnp.int32, (16, 2048), 0) + start == lane
        onehot_lanes[pl.ds(start, 16)] = jnp.where(hit, 1.0, 0.0).astype(jnp.bfloat16)
        for n in range(NT):
            onehot_lanes[pl.ds(128 * (1 + n) + start, 16)] = jnp.where(hit, high[n : n + 1], 0.0).astype(jnp.bfloat16)
            onehot_lanes[pl.ds(128 * (5 + n) + start, 16)] = jnp.where(hit, low[n : n + 1], 0.0).astype(jnp.bfloat16)
        return carry

    lax.fori_loop(0, 8, fill_lanes, 0)

    def spread(i, carry):
        start = pl.multiple_of(i * TILE, 16)
        product = lax.dot_general(
            onehot_rows[pl.ds(start, TILE)], onehot_lanes[...], (((1,), (1,)), ((), ())),
            preferred_element_type=jnp.float32,
        )
        counts[0, pl.ds(start, TILE)] = product[:, 0:128]
        for n in range(NT):
            counts[1 + n, pl.ds(start, TILE)] = (
                product[:, 128 * (1 + n) : 128 * (2 + n)] + product[:, 128 * (5 + n) : 128 * (6 + n)]
            )
        return carry

    for i in range(2):
        exchange[2 + i].wait_recv()
        opening[i].start()
    lax.fori_loop(0, LATER[0], spread, 0)
    exchange[5].wait_recv()
    pass_on(1)

    spot = source_ref[0]
    spot_plane = lax.shift_right_logical(spot, 16) - PLANES * slab
    spot_row = lax.bitwise_and(lax.shift_right_logical(spot, 7), 511) - SHIFT * h
    spot_lane = lax.bitwise_and(spot, 127)
    lanes = lax.broadcasted_iota(jnp.int32, (BLOCK, 128), 1)
    block_rows = lax.broadcasted_iota(jnp.int32, (BLOCK, 128), 0)
    first_lane = lanes == 0
    last_lane = lanes == 127

    def laplace(field, rim, p, r):
        middle = field[p, pl.ds(PAD + r, BLOCK)]
        if p < PLANES - 1:
            after = field[p + 1, pl.ds(PAD + r, BLOCK)]
        else:
            after = jnp.where(has_above, rim[1, pl.ds(r, BLOCK)], 0.0)
        if p > 0:
            prior = field[p - 1, pl.ds(PAD + r, BLOCK)]
        else:
            prior = jnp.where(has_below, rim[0, pl.ds(r, BLOCK)], 0.0)
        total = after + prior
        total = total + field[p, pl.ds(PAD + 1 + r, BLOCK)] + field[p, pl.ds(PAD - 1 + r, BLOCK)]
        total = total + jnp.where(last_lane, 0.0, pltpu.roll(middle, 127, 1))
        total = total + jnp.where(first_lane, 0.0, pltpu.roll(middle, 1, 1))
        return total - 6.0 * middle, middle

    def forward(n, planes, first, size):
        def block(i, carry):
            r = pl.multiple_of(first + i * BLOCK, 8)
            for p in planes:
                lap, middle = laplace(u.at[n + 1], halo.at[n], p, r)
                speed = model[p, pl.ds(r, BLOCK)]
                pulse = jnp.where(
                    (spot_plane == p) & (spot_lane == lanes) & (spot_row - r == block_rows), wavelet_ref[0, n], 0.0
                )
                after = 2.0 * middle - u[n, p, pl.ds(PAD + r, BLOCK)] + speed * lap + pulse
                u[n + 2, p, pl.ds(PAD + r, BLOCK)] = after
                if n < NT - 1:
                    laps[n, p, pl.ds(r, BLOCK)] = lap
                else:
                    miss = counts[0, pl.ds(p * ROWS + r, BLOCK)] * after - counts[NT, pl.ds(p * ROWS + r, BLOCK)]
                    adjoint[0, p, pl.ds(r, BLOCK)] = miss
                    weighted[0, p, pl.ds(PAD + r, BLOCK)] = speed * miss
                    image[int(p in OUTER), p // 2, pl.ds(r, BLOCK)] = miss * lap
            return carry

        lax.fori_loop(0, size // BLOCK, block, 0)

    def backward(j, planes, first, size):
        level = NT - 1 - j

        def block(i, carry):
            r = pl.multiple_of(first + i * BLOCK, 8)
            for p in planes:
                lap, _ = laplace(weighted.at[j], halo.at[NT + j], p, r)
                at = pl.ds(p * ROWS + r, BLOCK)
                miss = counts[0, at] * u[level + 1, p, pl.ds(PAD + r, BLOCK)] - counts[level, at]
                field = 2.0 * adjoint[j, p, pl.ds(r, BLOCK)] + lap + miss
                if j > 0:
                    field = field - adjoint[j - 1, p, pl.ds(r, BLOCK)]
                image[int(p in OUTER), p // 2, pl.ds(r, BLOCK)] += field * laps[level - 1, p, pl.ds(r, BLOCK)]
                if level > 1:
                    adjoint[j + 1, p, pl.ds(r, BLOCK)] = field
                    weighted[j + 1, p, pl.ds(PAD + r, BLOCK)] = model[p, pl.ds(r, BLOCK)] * field
            return carry

        lax.fori_loop(0, size // BLOCK, block, 0)

    def rim_copies(field, n, c):
        first, size = CHUNKS[c]
        at, to = pl.ds(PAD + first, size), pl.ds(first, size)
        return (
            copy_to(above, field.at[PLANES - 1, at], halo.at[n, 0, to], halo_send.at[n, c, 0], halo_recv.at[n, c, 0]),
            copy_to(below, field.at[0, at], halo.at[n, 1, to], halo_send.at[n, c, 1], halo_recv.at[n, c, 1]),
        )

    halos = []

    def send_rims(field, n, c):
        for copy in rim_copies(field, n, c):
            copy.start()
            halos.append(copy)

    for load in loads[2:]:
        load.wait()
    for i in (4, 1, 6):
        exchange[i].wait_recv()
    take_over(0)
    for copy in opening:
        copy.wait_recv()

    for n in range(NT):
        if n > 0:
            forward(n, INNER, 0, ROWS)
        for c, (first, size) in enumerate(CHUNKS):
            if n > 0:
                for copy in rim_copies(u.at[n + 1], n, c):
                    copy.wait_recv()
            forward(n, OUTER, first, size)
            if n < NT - 1:
                send_rims(u.at[n + 2], n + 1, c)
            else:
                send_rims(weighted.at[0], NT, c)
        if n == 0:
            exchange[7].wait_recv()
            take_over(1)
            forward(0, INNER, 0, ROWS)
        if n < NT - 1:
            lax.fori_loop(LATER[n], LATER[n + 1], spread, 0)

    half = pl.ds(pl.multiple_of(h * 256, 8), 256)
    kept = pl.ds(pl.multiple_of(PAD + 8 * h, 8), 256)
    store = pltpu.make_async_copy(u.at[NT + 1, own, kept], next_ref.at[0, :, half], next_sem.at[0])
    give = copy_to(pair, u.at[NT + 1, theirs, kept], next_ref.at[0, :, half], next_sem.at[1], next_sem.at[2])
    store.start()
    give.start()

    def band(j, parity):
        return pl.ds(pl.multiple_of(8 * h + 16 * (2 * j + parity), 8), 16)

    def core_copy(part, j):
        return copy_to(
            twin, image.at[part, :, band(j, 1 - core)], mate.at[part, j], core_send.at[part, j], core_recv.at[part, j]
        )

    def core_start(part):
        def step(j, carry):
            core_copy(part, j).start()
            return carry

        lax.fori_loop(0, 8, step, 0)

    def ring_copy(part, k):
        at, device = ring_device(k)
        src = shared.at[part, at // 2, lax.rem(at, 2)]
        return copy_to(device, src, crossed.at[part, x], ring_send.at[part, k], ring_recv.at[part, x])

    def core_finish(part):
        def step(j, carry):
            core_copy(part, j).wait_recv()
            shared[part, :, lax.rem(j, 2), j // 2] = image[part, :, band(j, core)] + mate[part, j]
            return carry

        lax.fori_loop(0, 8, step, 0)
        for k in range(1, 4):
            ring_copy(part, k).start()
        crossed[part, x] = shared[part, h, x_lo]

    def stack_copy(part, k):
        at, device = stack_device(k)
        return copy_to(device, gathered.at[part, at], landed.at[part, z], band_send.at[part, k], band_recv.at[part, z])

    def ring_finish(part):
        for k in range(1, 4):
            at, _ = ring_device(k)
            copy_to(twin, crossed.at[part, at], crossed.at[part, at], ring_send.at[part, k], ring_recv.at[part, at]).wait_recv()

        def step(j, carry):
            gathered[part, j] = crossed[part, 0, j] + crossed[part, 1, j]
            gathered[part, 4 + j] = crossed[part, 2, j] + crossed[part, 3, j]
            return carry

        lax.fori_loop(0, 4, step, 0)
        for k in range(1, 8):
            stack_copy(part, k).start()
        landed[part, z] = gathered[part, z]

    def stack_finish(part):
        for k in range(1, 8):
            at, _ = stack_device(k)
            copy_to(twin, landed.at[part, at], landed.at[part, at], band_send.at[part, k], band_recv.at[part, at]).wait_recv()
        total = landed[part, 0]
        for j in range(1, 8):
            total = total + landed[part, j]
        plane_at = h if part else 1 - h
        gradient_ref[plane_at] = total / NT - gradient_ref[plane_at]

    for j in range(NT - 1):
        backward(j, INNER, 0, ROWS)
        if j == NT - 2:
            core_start(0)
            core_finish(0)
        for c, (first, size) in enumerate(CHUNKS):
            for copy in rim_copies(weighted.at[j], NT + j, c):
                copy.wait_recv()
            backward(j, OUTER, first, size)
            if j < NT - 2:
                send_rims(weighted.at[j + 1], NT + j + 1, c)
    core_start(1)
    ring_finish(0)
    core_finish(1)

    for copy in rims:
        copy.wait_recv()

    band_lanes = lax.broadcasted_iota(jnp.int32, (16, 128), 1)
    start = pl.multiple_of(PAD + shot * 16, 8)
    for p in range(2):
        middle = kappa_rows[p, pl.ds(start, 16)]
        if p == 0:
            after = kappa_rows[1, pl.ds(start, 16)]
            prior = jnp.where(dom > 0, kappa_rim[0], 0.0)
        else:
            after = jnp.where(dom < 15, kappa_rim[1], 0.0)
            prior = kappa_rows[0, pl.ds(start, 16)]
        total = after + prior
        total = total + kappa_rows[p, pl.ds(start + 1, 16)] + kappa_rows[p, pl.ds(start - 1, 16)]
        total = total + jnp.where(band_lanes == 127, 0.0, pltpu.roll(middle, 127, 1))
        total = total + jnp.where(band_lanes == 0, 0.0, pltpu.roll(middle, 1, 1))
        gradient_ref[p] = (total / 6.0 - middle) * PRIOR_GAIN

    def sent(part):
        def step(j, carry):
            core_copy(part, j).wait_send()
            return carry

        lax.fori_loop(0, 8, step, 0)
        for k in range(1, 4):
            ring_copy(part, k).wait_send()

    for copy in exchange + passed + opening + rims + halos:
        copy.wait_send()
    store.wait()
    give.wait()
    sent(0)

    ring_finish(1)
    stack_finish(0)
    sent(1)
    for k in range(1, 8):
        stack_copy(0, k).wait_send()
    stack_finish(1)
    for k in range(1, 8):
        stack_copy(1, k).wait_send()


def hand_over(gradient_ref, next_ref, gradient_out, next_out, gradient, waves, load_sem, store_sem):
    loads, stores = [], []
    for p in range(2):
        for i in range(PIECES):
            rows = pl.ds(i * (512 // PIECES), 512 // PIECES)
            at = 1 + p * PIECES + i
            loads.append(pltpu.make_async_copy(next_ref.at[0, p, rows], waves.at[p, rows], load_sem.at[at]))
            stores.append(pltpu.make_async_copy(waves.at[p, rows], next_out.at[0, p, rows], store_sem.at[at]))
    loads.append(pltpu.make_async_copy(gradient_ref, gradient, load_sem.at[0]))
    stores.append(pltpu.make_async_copy(gradient, gradient_out, store_sem.at[0]))
    for load in loads:
        load.start()
    for load, store in zip(loads, stores):
        load.wait()
        store.start()
    for store in stores:
        store.wait()


def shards(kappa, wave_now, wave_before, wavelet, source_cell, receiver_cells, observed):
    f32 = jnp.float32
    chunks = len(CHUNKS)
    anywhere = pl.BlockSpec(memory_space=pl.ANY)
    vmem = pl.BlockSpec(memory_space=pltpu.VMEM)
    smem = pl.BlockSpec(memory_space=pltpu.SMEM)
    dma = pltpu.SemaphoreType.DMA
    results = pl.pallas_call(
        kernel,
        out_shape=(
            jax.ShapeDtypeStruct((2, 16, 128), f32),
            jax.ShapeDtypeStruct(wave_now.shape, f32),
        ),
        in_specs=[anywhere, anywhere, anywhere, smem, smem, anywhere, anywhere],
        out_specs=(vmem, anywhere),
        scratch_shapes=[
            pltpu.VMEM((6, PLANES, ROWS + 2 * PAD, 128), f32),
            pltpu.VMEM((PLANES, ROWS, 128), f32),
            pltpu.VMEM((3, PLANES, ROWS, 128), f32),
            pltpu.VMEM((5, CELL_ROWS, 128), f32),
            pltpu.VMEM((3, PLANES, ROWS, 128), f32),
            pltpu.VMEM((3, PLANES, ROWS + 2 * PAD, 128), f32),
            pltpu.VMEM((7, 2, ROWS, 128), f32),
            pltpu.VMEM((2, 2, ROWS, 128), f32),
            pltpu.VMEM((1, 2048), jnp.int32),
            pltpu.VMEM((1, NT, 2048), f32),
            pltpu.VMEM((CELL_ROWS, 2048), jnp.bfloat16),
            pltpu.VMEM((COLUMNS, 2048), jnp.bfloat16),
            pltpu.VMEM((2, 512 + 2 * PAD, 128), f32),
            pltpu.VMEM((2, 16, 128), f32),
            pltpu.VMEM((2, 8, 2, 16, 128), f32),
            pltpu.VMEM((2, 2, 2, 4, 16, 128), f32),
            pltpu.VMEM((2, 4, 4, 16, 128), f32),
            pltpu.VMEM((2, 8, 16, 128), f32),
            pltpu.VMEM((2, 8, 16, 128), f32),
            dma((6,)),
            dma((8,)),
            dma((8,)),
            dma((2, 8)),
            dma((2, 8)),
            dma((3,)),
            dma((3,)),
            dma((2,)),
            dma((2,)),
            dma((7, chunks, 2)),
            dma((7, chunks, 2)),
            dma((3,)),
            dma((2, 8)),
            dma((2, 8)),
            dma((2, 4)),
            dma((2, 4)),
            dma((2, 8)),
            dma((2, 8)),
        ],
        name="window",
        compiler_params=pltpu.CompilerParams(
            collective_id=0, has_side_effects=True, vmem_limit_bytes=56 << 20
        ),
    )(kappa, wave_now, wave_before, wavelet, source_cell, receiver_cells, observed)
    return pl.pallas_call(
        hand_over,
        out_shape=tuple(jax.ShapeDtypeStruct(r.shape, r.dtype) for r in results),
        in_specs=[anywhere, anywhere],
        out_specs=(anywhere, anywhere),
        scratch_shapes=[
            pltpu.VMEM((2, 16, 128), f32),
            pltpu.VMEM((2, 512, 128), f32),
            dma((1 + 2 * PIECES,)),
            dma((1 + 2 * PIECES,)),
        ],
        name="hand_over",
    )(*results)


def solution(mesh):
    return jax.shard_map(
        shards,
        mesh=mesh,
        in_specs=(
            P("dom", None, None),
            P("shot", "dom", None, None),
            P("shot", "dom", None, None),
            P("shot", None),
            P("shot"),
            P("shot", None),
            P("shot", None, None),
        ),
        out_specs=(P("dom", "shot", None), P("shot", "dom", None, None)),
        check_vma=False,
    )
```

```python
import jax
import jax.numpy as jnp
from jax import lax
from jax.experimental import pallas as pl
from jax.experimental.pallas import tpu as pltpu
from jax.sharding import PartitionSpec as P


NT = 4
PRIOR_GAIN = 50.0
PLANES = 4
ROWS = 264
SHIFT = 248
PAD = 8
BLOCK = 24
CHUNKS = ((0, 48), (48, 48), (96, 48), (144, 48), (192, 48), (240, 24))
HALVES = ((0, 144), (144, 120))
LAGGED = ((0, 24), (24, 48), (72, 48), (120, 48), (168, 48), (216, 48))
EARLY = 2
INNER = (1, 2)
OUTER = (0, 3)
CELL_ROWS = PLANES * ROWS
TILE = 352
COLUMNS = 9 * 128
PIECES = 2
MESH = pl.DeviceIdType.MESH


def kernel(
    kappa_ref, now_ref, before_ref, wavelet_ref, source_ref, receiver_ref, observed_ref,
    gradient_ref, next_ref,
    u, model, laps, counts, adjoint, weighted, halo, near, far, model_rim, image, cells, values_seen,
    onehot_rows, onehot_lanes, kappa_rows, kappa_rim, mate, shared, crossed, gathered, landed,
    local_sem, pair_send, pair_recv, share_send, share_recv, first_send, first_recv, lean_send, lean_recv, far_send, far_recv, rim_send, rim_recv, halo_send, halo_recv,
    next_sem, core_send, core_recv, ring_send, ring_recv, band_send, band_recv,
):
    shot = lax.axis_index("shot")
    dom = lax.axis_index("dom")
    h = lax.rem(dom, 2)
    slab = dom // 2
    core = lax.rem(shot, 2)
    x_lo = lax.rem(shot // 2, 2)
    z = shot // 4
    pair = (shot, dom + 1 - 2 * h)
    above = (shot, lax.rem(dom + 2, 16))
    below = (shot, lax.rem(dom + 14, 16))
    next_dom = (shot, lax.rem(dom + 1, 16))
    last_dom = (shot, lax.rem(dom + 15, 16))
    other = (shot, lax.rem(dom + 15 + 2 * h, 16))
    twin = (shot + 1 - 2 * core, dom)
    x = 2 * h + x_lo
    has_below = slab > 0
    has_above = slab < 7

    def copy_to(device, src, dst, send, recv):
        return pltpu.make_async_remote_copy(
            src_ref=src, dst_ref=dst, send_sem=send, recv_sem=recv, device_id=device, device_id_type=MESH
        )

    def ring_device(k):
        at = lax.rem(x + k, 4)
        return at, (z * 4 + lax.rem(at, 2) * 2 + core, 2 * slab + at // 2)

    def stack_device(k):
        at = lax.rem(z + k, 8)
        return at, (at * 4 + x_lo * 2 + core, dom)

    mine_rows = pl.ds(pl.multiple_of(h * SHIFT, 8), ROWS)
    pair_rows = pl.ds(pl.multiple_of((1 - h) * SHIFT, 8), ROWS)
    own = pl.ds(2 * h, 2)
    theirs = pl.ds(2 - 2 * h, 2)
    body = pl.ds(PAD, ROWS)

    barrier = pltpu.get_barrier_semaphore()
    greeted = [pair, above, below, other, twin, ring_device(1)[1], ring_device(3)[1]]
    greeted += [stack_device(k)[1] for k in range(1, 8)]
    for device in greeted:
        pl.semaphore_signal(barrier, inc=1, device_id=device, device_id_type=MESH)

    loads = [
        pltpu.make_async_copy(receiver_ref, cells, local_sem.at[4]),
        pltpu.make_async_copy(observed_ref, values_seen, local_sem.at[5]),
        pltpu.make_async_copy(now_ref.at[0, :, mine_rows], u.at[1, own, body], local_sem.at[0]),
        pltpu.make_async_copy(kappa_ref.at[:, mine_rows], model.at[own], local_sem.at[1]),
        pltpu.make_async_copy(before_ref.at[0, :, mine_rows], u.at[0, own, body], local_sem.at[2]),
        pltpu.make_async_copy(kappa_ref, kappa_rows.at[:, pl.ds(PAD, 512)], local_sem.at[3]),
    ]
    for load in loads:
        load.start()
    for n in range(6):
        for p in range(PLANES):
            u[n, p, 0:PAD] = jnp.zeros((PAD, 128), jnp.float32)
            u[n, p, PAD + ROWS : 2 * PAD + ROWS] = jnp.zeros((PAD, 128), jnp.float32)
    for n in range(3):
        for p in range(PLANES):
            weighted[n, p, 0:PAD] = jnp.zeros((PAD, 128), jnp.float32)
            weighted[n, p, PAD + ROWS : 2 * PAD + ROWS] = jnp.zeros((PAD, 128), jnp.float32)
    for p in range(2):
        near[p, 0:PAD] = jnp.zeros((PAD, 128), jnp.float32)
        near[p, PAD + ROWS : 2 * PAD + ROWS] = jnp.zeros((PAD, 128), jnp.float32)
        kappa_rows[p, 0:PAD] = jnp.zeros((PAD, 128), jnp.float32)
        kappa_rows[p, PAD + 512 : 2 * PAD + 512] = jnp.zeros((PAD, 128), jnp.float32)

    loads[0].wait()
    cell = cells[...]
    plane = lax.shift_right_logical(cell, 16) - PLANES * slab
    row = lax.bitwise_and(lax.shift_right_logical(cell, 7), 511) - SHIFT * h
    inside = (plane >= 0) & (plane < PLANES) & (row >= 0) & (row < ROWS)
    cell_row = jnp.where(inside, plane * ROWS + row, -1)
    lane = lax.bitwise_and(cell, 127)

    def fill_rows(i, carry):
        start = pl.multiple_of(i * 16, 16)
        ids = lax.broadcasted_iota(jnp.int32, (16, 2048), 0) + start
        onehot_rows[pl.ds(start, 16)] = jnp.where(ids == cell_row, 1.0, 0.0).astype(jnp.bfloat16)
        return carry

    lax.fori_loop(0, CELL_ROWS // 16, fill_rows, 0)
    pl.semaphore_wait(barrier, len(greeted))

    def share(first, size):
        return pl.ds(pl.multiple_of(first, 8), size)

    eighth = share(z * 32, 32)

    def outer_copy(i):
        first, size = HALVES[i]
        src = now_ref.at[0, h, share((1 - h) * SHIFT + first, size)]
        return copy_to(pair, src, u.at[1, 3 * h, pl.ds(PAD + first, size)], pair_send.at[4 + i], pair_recv.at[4 + i])

    def relay(i):
        first, size = HALVES[i]
        device = (shot, lax.rem(dom + 2 + 12 * h, 16))
        src = u.at[1, 3 - 3 * h, pl.ds(PAD + first, size)]
        return copy_to(device, src, halo.at[0, h, pl.ds(first, size)], first_send.at[i], first_recv.at[i])

    direct = copy_to(
        (shot, lax.rem(dom + 14 + 4 * h, 16)), now_ref.at[0, h, mine_rows], halo.at[0, 1 - h], first_send.at[2], first_recv.at[2]
    )
    opening = [relay(0), relay(1), direct]
    lean = [
        copy_to(
            (shot, lax.rem(dom + 14 + 4 * h, 16)), kappa_ref.at[h, mine_rows], model_rim.at[1 - h], lean_send.at[0], lean_recv.at[0]
        ),
        copy_to((shot, lax.rem(dom + 2 + 12 * h, 16)), model.at[3 - 3 * h], model_rim.at[h], lean_send.at[1], lean_recv.at[1]),
    ]

    def kappa_copy(i):
        src = kappa_ref.at[(h, 1 - h)[i], share((1 - h) * SHIFT + z * 32, 32)]
        return copy_to(pair, src, model.at[(3 * h, 1 + h)[i], eighth], pair_send.at[i], pair_recv.at[i])

    def before_copy(i):
        src = before_ref.at[0, (h, 1 - h)[i], pair_rows]
        return copy_to(pair, src, u.at[0, (3 * h, 1 + h)[i], body], pair_send.at[6 + i], pair_recv.at[6 + i])

    exchange = [
        kappa_copy(0),
        copy_to(
            pair, kappa_ref.at[:, share((1 - h) * SHIFT + 256, 8)], model.at[own, 256:264], pair_send.at[2], pair_recv.at[2]
        ),
        outer_copy(0),
        outer_copy(1),
        copy_to(pair, now_ref.at[0, 1 - h, pair_rows], u.at[1, 1 + h, body], pair_send.at[3], pair_recv.at[3]),
        kappa_copy(1),
        before_copy(0),
        before_copy(1),
    ]
    direct.start()
    lean[0].start()
    for copy in exchange:
        copy.start()
    band_rows = pl.ds(pl.multiple_of(shot * 16, 8), 16)
    rims = [
        copy_to(next_dom, kappa_ref.at[1, band_rows], kappa_rim.at[0], rim_send.at[0], rim_recv.at[0]),
        copy_to(last_dom, kappa_ref.at[0, band_rows], kappa_rim.at[1], rim_send.at[1], rim_recv.at[1]),
    ]
    for copy in rims:
        copy.start()

    passed = []

    def pass_on(i):
        part = model.at[(3 - 3 * h, 2 - h)[i], eighth]
        for k in range(1, 8):
            copy = copy_to(stack_device(k)[1], part, part, share_send.at[i, k], share_recv.at[i, z])
            copy.start()
            passed.append(copy)

    def take_over(i):
        for k in range(1, 8):
            at, device = stack_device(k)
            part = model.at[(3 - 3 * h, 2 - h)[i], share(at * 32, 32)]
            copy_to(device, part, part, share_send.at[i, k], share_recv.at[i, at]).wait_recv()

    exchange[0].wait_recv()
    pass_on(0)

    loads[1].wait()
    values = values_seen[0]
    high = values.astype(jnp.bfloat16).astype(jnp.float32)
    low = values - high

    def fill_lanes(i, carry):
        start = pl.multiple_of(i * 16, 16)
        hit = lax.broadcasted_iota(jnp.int32, (16, 2048), 0) + start == lane
        onehot_lanes[pl.ds(start, 16)] = jnp.where(hit, 1.0, 0.0).astype(jnp.bfloat16)
        for n in range(NT):
            onehot_lanes[pl.ds(128 * (1 + n) + start, 16)] = jnp.where(hit, high[n : n + 1], 0.0).astype(jnp.bfloat16)
            onehot_lanes[pl.ds(128 * (5 + n) + start, 16)] = jnp.where(hit, low[n : n + 1], 0.0).astype(jnp.bfloat16)
        return carry

    lax.fori_loop(0, 8, fill_lanes, 0)

    def spread(i, carry):
        start = pl.multiple_of(i * TILE, 16)
        product = lax.dot_general(
            onehot_rows[pl.ds(start, TILE)], onehot_lanes[...], (((1,), (1,)), ((), ())),
            preferred_element_type=jnp.float32,
        )
        counts[0, pl.ds(start, TILE)] = product[:, 0:128]
        for n in range(NT):
            counts[1 + n, pl.ds(start, TILE)] = (
                product[:, 128 * (1 + n) : 128 * (2 + n)] + product[:, 128 * (5 + n) : 128 * (6 + n)]
            )
        return carry

    for i in range(2):
        exchange[2 + i].wait_recv()
        opening[i].start()
    lax.fori_loop(0, EARLY, spread, 0)
    exchange[5].wait_recv()
    pass_on(1)

    spot = source_ref[0]
    spot_plane = lax.shift_right_logical(spot, 16) - PLANES * slab
    spot_row = lax.bitwise_and(lax.shift_right_logical(spot, 7), 511) - SHIFT * h
    spot_lane = lax.bitwise_and(spot, 127)
    lanes = lax.broadcasted_iota(jnp.int32, (BLOCK, 128), 1)
    block_rows = lax.broadcasted_iota(jnp.int32, (BLOCK, 128), 0)
    first_lane = lanes == 0
    last_lane = lanes == 127

    def laplace(field, rim, p, r):
        middle = field[p, pl.ds(PAD + r, BLOCK)]
        if p < PLANES - 1:
            after = field[p + 1, pl.ds(PAD + r, BLOCK)]
        else:
            after = jnp.where(has_above, rim[1][pl.ds(r, BLOCK)], 0.0)
        if p > 0:
            prior = field[p - 1, pl.ds(PAD + r, BLOCK)]
        else:
            prior = jnp.where(has_below, rim[0][pl.ds(r, BLOCK)], 0.0)
        total = after + prior
        total = total + field[p, pl.ds(PAD + 1 + r, BLOCK)] + field[p, pl.ds(PAD - 1 + r, BLOCK)]
        total = total + jnp.where(last_lane, 0.0, pltpu.roll(middle, 127, 1))
        total = total + jnp.where(first_lane, 0.0, pltpu.roll(middle, 1, 1))
        return total - 6.0 * middle, middle

    def rims_of(n):
        if n == 2:
            return near.at[0, pl.ds(PAD, ROWS)], near.at[1, pl.ds(PAD, ROWS)]
        return halo.at[n, 0], halo.at[n, 1]

    def edge(first, size):
        def block(i, carry):
            r = pl.multiple_of(first + i * BLOCK, 8)
            for side in range(2):
                middle = near[side, pl.ds(PAD + r, BLOCK)]
                total = far[side, pl.ds(r, BLOCK)] + u[3, 3 * side, pl.ds(PAD + r, BLOCK)]
                total = total + near[side, pl.ds(PAD + 1 + r, BLOCK)] + near[side, pl.ds(PAD - 1 + r, BLOCK)]
                total = total + jnp.where(last_lane, 0.0, pltpu.roll(middle, 127, 1))
                total = total + jnp.where(first_lane, 0.0, pltpu.roll(middle, 1, 1))
                lap = total - 6.0 * middle
                hit = (spot_plane == 5 * side - 1) & (spot_lane == lanes) & (spot_row - r == block_rows)
                pulse = jnp.where(hit, wavelet_ref[0, 2], 0.0)
                halo[3, side, pl.ds(r, BLOCK)] = (
                    2.0 * middle - halo[1, side, pl.ds(r, BLOCK)] + model_rim[side, pl.ds(r, BLOCK)] * lap + pulse
                )
            return carry

        lax.fori_loop(0, size // BLOCK, block, 0)

    def forward(n, planes, first, size):
        def block(i, carry):
            r = pl.multiple_of(first + i * BLOCK, 8)
            for p in planes:
                lap, middle = laplace(u.at[n + 1], rims_of(n), p, r)
                speed = model[p, pl.ds(r, BLOCK)]
                pulse = jnp.where(
                    (spot_plane == p) & (spot_lane == lanes) & (spot_row - r == block_rows), wavelet_ref[0, n], 0.0
                )
                after = 2.0 * middle - u[n, p, pl.ds(PAD + r, BLOCK)] + speed * lap + pulse
                u[n + 2, p, pl.ds(PAD + r, BLOCK)] = after
                if n < NT - 1:
                    laps[n, p, pl.ds(r, BLOCK)] = lap
                else:
                    miss = counts[0, pl.ds(p * ROWS + r, BLOCK)] * after - counts[NT, pl.ds(p * ROWS + r, BLOCK)]
                    adjoint[0, p, pl.ds(r, BLOCK)] = miss
                    weighted[0, p, pl.ds(PAD + r, BLOCK)] = speed * miss
                    image[int(p in OUTER), p // 2, pl.ds(r, BLOCK)] = miss * lap
            return carry

        lax.fori_loop(0, size // BLOCK, block, 0)

    def backward(j, planes, first, size):
        level = NT - 1 - j

        def block(i, carry):
            r = pl.multiple_of(first + i * BLOCK, 8)
            for p in planes:
                lap, _ = laplace(weighted.at[j], rims_of(NT + j), p, r)
                at = pl.ds(p * ROWS + r, BLOCK)
                miss = counts[0, at] * u[level + 1, p, pl.ds(PAD + r, BLOCK)] - counts[level, at]
                field = 2.0 * adjoint[j, p, pl.ds(r, BLOCK)] + lap + miss
                if j > 0:
                    field = field - adjoint[j - 1, p, pl.ds(r, BLOCK)]
                image[int(p in OUTER), p // 2, pl.ds(r, BLOCK)] += field * laps[level - 1, p, pl.ds(r, BLOCK)]
                if level > 1:
                    adjoint[j + 1, p, pl.ds(r, BLOCK)] = field
                    weighted[j + 1, p, pl.ds(PAD + r, BLOCK)] = model[p, pl.ds(r, BLOCK)] * field
            return carry

        lax.fori_loop(0, size // BLOCK, block, 0)

    def rim_copies(field, n, c):
        first, size = LAGGED[c] if n >= NT else CHUNKS[c]
        at, to = pl.ds(PAD + first, size), pl.ds(first, size)
        into = (near.at[0, at], near.at[1, at]) if n == 2 else (halo.at[n, 0, to], halo.at[n, 1, to])
        return (
            copy_to(above, field.at[PLANES - 1, at], into[0], halo_send.at[n, c, 0], halo_recv.at[n, c, 0]),
            copy_to(below, field.at[0, at], into[1], halo_send.at[n, c, 1], halo_recv.at[n, c, 1]),
        )

    def far_copies(i):
        first, size = HALVES[i]
        at, to = pl.ds(PAD + first, size), pl.ds(first, size)
        return (
            copy_to(above, u.at[3, 2, at], far.at[0, to], far_send.at[i, 0], far_recv.at[i, 0]),
            copy_to(below, u.at[3, 1, at], far.at[1, to], far_send.at[i, 1], far_recv.at[i, 1]),
        )

    halos = []

    def send_rims(field, n, c):
        for copy in rim_copies(field, n, c):
            copy.start()
            halos.append(copy)

    for load in loads[2:]:
        load.wait()
    for i in (4, 1, 6):
        exchange[i].wait_recv()
    take_over(0)
    for copy in opening:
        copy.wait_recv()

    for c, (first, size) in enumerate(CHUNKS):
        forward(0, OUTER, first, size)
        send_rims(u.at[2], 1, c)
    lean[1].start()
    exchange[7].wait_recv()
    take_over(1)
    forward(0, INNER, 0, ROWS)

    forward(1, INNER, 0, ROWS)
    for i in range(2):
        for copy in far_copies(i):
            copy.start()
            halos.append(copy)
    lax.fori_loop(EARLY, CELL_ROWS // TILE, spread, 0)
    for c, (first, size) in enumerate(CHUNKS):
        for copy in rim_copies(u.at[2], 1, c):
            copy.wait_recv()
        forward(1, OUTER, first, size)
        send_rims(u.at[3], 2, c)

    forward(2, INNER, 0, ROWS)
    for copy in lean:
        copy.wait_recv()
    for i in range(2):
        for copy in far_copies(i):
            copy.wait_recv()
    for c, (first, size) in enumerate(CHUNKS):
        for copy in rim_copies(u.at[3], 2, c):
            copy.wait_recv()
        forward(2, OUTER, first, size)
        edge(*LAGGED[c])
        forward(3, OUTER, *LAGGED[c])
        send_rims(weighted.at[0], NT, c)
    forward(3, INNER, 0, ROWS)

    half = pl.ds(pl.multiple_of(h * 256, 8), 256)
    kept = pl.ds(pl.multiple_of(PAD + 8 * h, 8), 256)
    store = pltpu.make_async_copy(u.at[NT + 1, own, kept], next_ref.at[0, :, half], next_sem.at[0])
    give = copy_to(pair, u.at[NT + 1, theirs, kept], next_ref.at[0, :, half], next_sem.at[1], next_sem.at[2])
    store.start()
    give.start()

    def band(j, parity):
        return pl.ds(pl.multiple_of(8 * h + 16 * (2 * j + parity), 8), 16)

    def core_copy(part, j):
        return copy_to(
            twin, image.at[part, :, band(j, 1 - core)], mate.at[part, j], core_send.at[part, j], core_recv.at[part, j]
        )

    def core_start(part):
        def step(j, carry):
            core_copy(part, j).start()
            return carry

        lax.fori_loop(0, 8, step, 0)

    def ring_copy(part, k):
        at, device = ring_device(k)
        src = shared.at[part, at // 2, lax.rem(at, 2)]
        return copy_to(device, src, crossed.at[part, x], ring_send.at[part, k], ring_recv.at[part, x])

    def core_finish(part):
        def step(j, carry):
            core_copy(part, j).wait_recv()
            shared[part, :, lax.rem(j, 2), j // 2] = image[part, :, band(j, core)] + mate[part, j]
            return carry

        lax.fori_loop(0, 8, step, 0)
        for k in range(1, 4):
            ring_copy(part, k).start()
        crossed[part, x] = shared[part, h, x_lo]

    def stack_copy(part, k):
        at, device = stack_device(k)
        return copy_to(device, gathered.at[part, at], landed.at[part, z], band_send.at[part, k], band_recv.at[part, z])

    def ring_finish(part):
        for k in range(1, 4):
            at, _ = ring_device(k)
            copy_to(twin, crossed.at[part, at], crossed.at[part, at], ring_send.at[part, k], ring_recv.at[part, at]).wait_recv()

        def step(j, carry):
            gathered[part, j] = crossed[part, 0, j] + crossed[part, 1, j]
            gathered[part, 4 + j] = crossed[part, 2, j] + crossed[part, 3, j]
            return carry

        lax.fori_loop(0, 4, step, 0)
        for k in range(1, 8):
            stack_copy(part, k).start()
        landed[part, z] = gathered[part, z]

    def stack_finish(part):
        for k in range(1, 8):
            at, _ = stack_device(k)
            copy_to(twin, landed.at[part, at], landed.at[part, at], band_send.at[part, k], band_recv.at[part, at]).wait_recv()
        total = landed[part, 0]
        for j in range(1, 8):
            total = total + landed[part, j]
        plane_at = h if part else 1 - h
        gradient_ref[plane_at] = total / NT - gradient_ref[plane_at]

    for j in range(NT - 1):
        backward(j, INNER, 0, ROWS)
        if j == NT - 2:
            core_start(0)
            core_finish(0)
        for c, (first, size) in enumerate(LAGGED):
            for copy in rim_copies(weighted.at[j], NT + j, c):
                copy.wait_recv()
            backward(j, OUTER, first, size)
            if j < NT - 2:
                send_rims(weighted.at[j + 1], NT + j + 1, c)
    core_start(1)
    ring_finish(0)
    core_finish(1)

    for copy in rims:
        copy.wait_recv()

    band_lanes = lax.broadcasted_iota(jnp.int32, (16, 128), 1)
    start = pl.multiple_of(PAD + shot * 16, 8)
    for p in range(2):
        middle = kappa_rows[p, pl.ds(start, 16)]
        if p == 0:
            after = kappa_rows[1, pl.ds(start, 16)]
            prior = jnp.where(dom > 0, kappa_rim[0], 0.0)
        else:
            after = jnp.where(dom < 15, kappa_rim[1], 0.0)
            prior = kappa_rows[0, pl.ds(start, 16)]
        total = after + prior
        total = total + kappa_rows[p, pl.ds(start + 1, 16)] + kappa_rows[p, pl.ds(start - 1, 16)]
        total = total + jnp.where(band_lanes == 127, 0.0, pltpu.roll(middle, 127, 1))
        total = total + jnp.where(band_lanes == 0, 0.0, pltpu.roll(middle, 1, 1))
        gradient_ref[p] = (total / 6.0 - middle) * PRIOR_GAIN

    def sent(part):
        def step(j, carry):
            core_copy(part, j).wait_send()
            return carry

        lax.fori_loop(0, 8, step, 0)
        for k in range(1, 4):
            ring_copy(part, k).wait_send()

    for copy in exchange + passed + opening + lean + rims + halos:
        copy.wait_send()
    store.wait()
    give.wait()
    sent(0)

    ring_finish(1)
    stack_finish(0)
    sent(1)
    for k in range(1, 8):
        stack_copy(0, k).wait_send()
    stack_finish(1)
    for k in range(1, 8):
        stack_copy(1, k).wait_send()


def hand_over(gradient_ref, next_ref, gradient_out, next_out, gradient, waves, load_sem, store_sem):
    loads, stores = [], []
    for p in range(2):
        for i in range(PIECES):
            rows = pl.ds(i * (512 // PIECES), 512 // PIECES)
            at = 1 + p * PIECES + i
            loads.append(pltpu.make_async_copy(next_ref.at[0, p, rows], waves.at[p, rows], load_sem.at[at]))
            stores.append(pltpu.make_async_copy(waves.at[p, rows], next_out.at[0, p, rows], store_sem.at[at]))
    loads.append(pltpu.make_async_copy(gradient_ref, gradient, load_sem.at[0]))
    stores.append(pltpu.make_async_copy(gradient, gradient_out, store_sem.at[0]))
    for load in loads:
        load.start()
    for load, store in zip(loads, stores):
        load.wait()
        store.start()
    for store in stores:
        store.wait()


def shards(kappa, wave_now, wave_before, wavelet, source_cell, receiver_cells, observed):
    f32 = jnp.float32
    chunks = len(CHUNKS)
    anywhere = pl.BlockSpec(memory_space=pl.ANY)
    vmem = pl.BlockSpec(memory_space=pltpu.VMEM)
    smem = pl.BlockSpec(memory_space=pltpu.SMEM)
    dma = pltpu.SemaphoreType.DMA
    results = pl.pallas_call(
        kernel,
        out_shape=(
            jax.ShapeDtypeStruct((2, 16, 128), f32),
            jax.ShapeDtypeStruct(wave_now.shape, f32),
        ),
        in_specs=[anywhere, anywhere, anywhere, smem, smem, anywhere, anywhere],
        out_specs=(vmem, anywhere),
        scratch_shapes=[
            pltpu.VMEM((6, PLANES, ROWS + 2 * PAD, 128), f32),
            pltpu.VMEM((PLANES, ROWS, 128), f32),
            pltpu.VMEM((3, PLANES, ROWS, 128), f32),
            pltpu.VMEM((5, CELL_ROWS, 128), f32),
            pltpu.VMEM((3, PLANES, ROWS, 128), f32),
            pltpu.VMEM((3, PLANES, ROWS + 2 * PAD, 128), f32),
            pltpu.VMEM((7, 2, ROWS, 128), f32),
            pltpu.VMEM((2, ROWS + 2 * PAD, 128), f32),
            pltpu.VMEM((2, ROWS, 128), f32),
            pltpu.VMEM((2, ROWS, 128), f32),
            pltpu.VMEM((2, 2, ROWS, 128), f32),
            pltpu.VMEM((1, 2048), jnp.int32),
            pltpu.VMEM((1, NT, 2048), f32),
            pltpu.VMEM((CELL_ROWS, 2048), jnp.bfloat16),
            pltpu.VMEM((COLUMNS, 2048), jnp.bfloat16),
            pltpu.VMEM((2, 512 + 2 * PAD, 128), f32),
            pltpu.VMEM((2, 16, 128), f32),
            pltpu.VMEM((2, 8, 2, 16, 128), f32),
            pltpu.VMEM((2, 2, 2, 4, 16, 128), f32),
            pltpu.VMEM((2, 4, 4, 16, 128), f32),
            pltpu.VMEM((2, 8, 16, 128), f32),
            pltpu.VMEM((2, 8, 16, 128), f32),
            dma((6,)),
            dma((8,)),
            dma((8,)),
            dma((2, 8)),
            dma((2, 8)),
            dma((3,)),
            dma((3,)),
            dma((2,)),
            dma((2,)),
            dma((2, 2)),
            dma((2, 2)),
            dma((2,)),
            dma((2,)),
            dma((7, chunks, 2)),
            dma((7, chunks, 2)),
            dma((3,)),
            dma((2, 8)),
            dma((2, 8)),
            dma((2, 4)),
            dma((2, 4)),
            dma((2, 8)),
            dma((2, 8)),
        ],
        name="window",
        compiler_params=pltpu.CompilerParams(
            collective_id=0, has_side_effects=True, vmem_limit_bytes=56 << 20
        ),
    )(kappa, wave_now, wave_before, wavelet, source_cell, receiver_cells, observed)
    return pl.pallas_call(
        hand_over,
        out_shape=tuple(jax.ShapeDtypeStruct(r.shape, r.dtype) for r in results),
        in_specs=[anywhere, anywhere],
        out_specs=(anywhere, anywhere),
        scratch_shapes=[
            pltpu.VMEM((2, 16, 128), f32),
            pltpu.VMEM((2, 512, 128), f32),
            dma((1 + 2 * PIECES,)),
            dma((1 + 2 * PIECES,)),
        ],
        name="hand_over",
    )(*results)


def solution(mesh):
    return jax.shard_map(
        shards,
        mesh=mesh,
        in_specs=(
            P("dom", None, None),
            P("shot", "dom", None, None),
            P("shot", "dom", None, None),
            P("shot", None),
            P("shot"),
            P("shot", None),
            P("shot", None, None),
        ),
        out_specs=(P("dom", "shot", None), P("shot", "dom", None, None)),
        check_vma=False,
    )
```

```python
import jax
import jax.numpy as jnp
from jax import lax
from jax.experimental import pallas as pl
from jax.experimental.pallas import tpu as pltpu
from jax.sharding import PartitionSpec as P


NT = 4
PRIOR_GAIN = 50.0
PLANES = 4
ROWS = 264
SHIFT = 248
PAD = 8
BLOCK = 24
CHUNKS = ((0, 48), (48, 48), (96, 48), (144, 48), (192, 48), (240, 24))
HALVES = ((0, 144), (144, 120))
LAGGED = ((0, 24), (24, 48), (72, 48), (120, 48), (168, 48), (216, 48))
EARLY = 2
INNER = (1, 2)
OUTER = (0, 3)
CELL_ROWS = PLANES * ROWS
TILE = 352
COLUMNS = 9 * 128
PIECES = 2
MESH = pl.DeviceIdType.MESH


def kernel(
    kappa_ref, now_ref, before_ref, wavelet_ref, source_ref, receiver_ref, observed_ref,
    gradient_ref, next_ref,
    u, model, laps, counts, adjoint, weighted, halo, near, far, model_rim, image, cells, values_seen,
    onehot_rows, onehot_lanes, kappa_rows, kappa_rim, mate, shared, crossed, gathered, landed,
    local_sem, pair_send, pair_recv, share_send, share_recv, first_send, first_recv, lean_send, lean_recv, far_send, far_recv, rim_send, rim_recv, halo_send, halo_recv,
    next_sem, core_send, core_recv, ring_send, ring_recv, band_send, band_recv,
):
    shot = lax.axis_index("shot")
    dom = lax.axis_index("dom")
    h = lax.rem(dom, 2)
    slab = dom // 2
    core = lax.rem(shot, 2)
    x_lo = lax.rem(shot // 2, 2)
    z = shot // 4
    pair = (shot, dom + 1 - 2 * h)
    above = (shot, lax.rem(dom + 2, 16))
    below = (shot, lax.rem(dom + 14, 16))
    next_dom = (shot, lax.rem(dom + 1, 16))
    last_dom = (shot, lax.rem(dom + 15, 16))
    other = (shot, lax.rem(dom + 15 + 2 * h, 16))
    twin = (shot + 1 - 2 * core, dom)
    x = 2 * h + x_lo
    has_below = slab > 0
    has_above = slab < 7

    def copy_to(device, src, dst, send, recv):
        return pltpu.make_async_remote_copy(
            src_ref=src, dst_ref=dst, send_sem=send, recv_sem=recv, device_id=device, device_id_type=MESH
        )

    def ring_device(k):
        at = lax.rem(x + k, 4)
        return at, (z * 4 + lax.rem(at, 2) * 2 + core, 2 * slab + at // 2)

    def stack_device(k):
        at = lax.rem(z + k, 8)
        return at, (at * 4 + x_lo * 2 + core, dom)

    mine_rows = pl.ds(pl.multiple_of(h * SHIFT, 8), ROWS)
    pair_rows = pl.ds(pl.multiple_of((1 - h) * SHIFT, 8), ROWS)
    own = pl.ds(2 * h, 2)
    theirs = pl.ds(2 - 2 * h, 2)
    body = pl.ds(PAD, ROWS)

    barrier = pltpu.get_barrier_semaphore()
    greeted = [pair, above, below, other, twin, ring_device(1)[1], ring_device(3)[1]]
    greeted += [stack_device(k)[1] for k in range(1, 8)]
    for device in greeted:
        pl.semaphore_signal(barrier, inc=1, device_id=device, device_id_type=MESH)

    loads = [
        pltpu.make_async_copy(receiver_ref, cells, local_sem.at[4]),
        pltpu.make_async_copy(observed_ref, values_seen, local_sem.at[5]),
        pltpu.make_async_copy(now_ref.at[0, :, mine_rows], u.at[1, own, body], local_sem.at[0]),
        pltpu.make_async_copy(kappa_ref.at[:, mine_rows], model.at[own], local_sem.at[1]),
        pltpu.make_async_copy(before_ref.at[0, :, mine_rows], u.at[0, own, body], local_sem.at[2]),
        pltpu.make_async_copy(kappa_ref, kappa_rows.at[:, pl.ds(PAD, 512)], local_sem.at[3]),
    ]
    for load in loads:
        load.start()
    for n in range(6):
        for p in range(PLANES):
            u[n, p, 0:PAD] = jnp.zeros((PAD, 128), jnp.float32)
            u[n, p, PAD + ROWS : 2 * PAD + ROWS] = jnp.zeros((PAD, 128), jnp.float32)
    for n in range(3):
        for p in range(PLANES):
            weighted[n, p, 0:PAD] = jnp.zeros((PAD, 128), jnp.float32)
            weighted[n, p, PAD + ROWS : 2 * PAD + ROWS] = jnp.zeros((PAD, 128), jnp.float32)
    for p in range(2):
        near[p, 0:PAD] = jnp.zeros((PAD, 128), jnp.float32)
        near[p, PAD + ROWS : 2 * PAD + ROWS] = jnp.zeros((PAD, 128), jnp.float32)
        kappa_rows[p, 0:PAD] = jnp.zeros((PAD, 128), jnp.float32)
        kappa_rows[p, PAD + 512 : 2 * PAD + 512] = jnp.zeros((PAD, 128), jnp.float32)

    loads[0].wait()
    cell = cells[...]
    plane = lax.shift_right_logical(cell, 16) - PLANES * slab
    row = lax.bitwise_and(lax.shift_right_logical(cell, 7), 511) - SHIFT * h
    inside = (plane >= 0) & (plane < PLANES) & (row >= 0) & (row < ROWS)
    cell_row = jnp.where(inside, plane * ROWS + row, -1)
    lane = lax.bitwise_and(cell, 127)

    def fill_rows(i, carry):
        start = pl.multiple_of(i * 16, 16)
        ids = lax.broadcasted_iota(jnp.int32, (16, 2048), 0) + start
        onehot_rows[pl.ds(start, 16)] = jnp.where(ids == cell_row, 1.0, 0.0).astype(jnp.bfloat16)
        return carry

    lax.fori_loop(0, CELL_ROWS // 16, fill_rows, 0)
    pl.semaphore_wait(barrier, len(greeted))

    def share(first, size):
        return pl.ds(pl.multiple_of(first, 8), size)

    eighth = share(z * 32, 32)

    def outer_copy(i):
        first, size = HALVES[i]
        src = now_ref.at[0, h, share((1 - h) * SHIFT + first, size)]
        return copy_to(pair, src, u.at[1, 3 * h, pl.ds(PAD + first, size)], pair_send.at[4 + i], pair_recv.at[4 + i])

    def relay(i):
        first, size = HALVES[i]
        device = (shot, lax.rem(dom + 2 + 12 * h, 16))
        src = u.at[1, 3 - 3 * h, pl.ds(PAD + first, size)]
        return copy_to(device, src, halo.at[0, h, pl.ds(first, size)], first_send.at[i], first_recv.at[i])

    direct = copy_to(
        (shot, lax.rem(dom + 14 + 4 * h, 16)), now_ref.at[0, h, mine_rows], halo.at[0, 1 - h], first_send.at[2], first_recv.at[2]
    )
    opening = [relay(0), relay(1), direct]
    lean = [
        copy_to(
            (shot, lax.rem(dom + 14 + 4 * h, 16)), kappa_ref.at[h, mine_rows], model_rim.at[1 - h], lean_send.at[0], lean_recv.at[0]
        ),
        copy_to((shot, lax.rem(dom + 2 + 12 * h, 16)), model.at[3 - 3 * h], model_rim.at[h], lean_send.at[1], lean_recv.at[1]),
    ]

    def kappa_copy(i):
        src = kappa_ref.at[(h, 1 - h)[i], share((1 - h) * SHIFT + z * 32, 32)]
        return copy_to(pair, src, model.at[(3 * h, 1 + h)[i], eighth], pair_send.at[i], pair_recv.at[i])

    def before_copy(i):
        src = before_ref.at[0, (h, 1 - h)[i], pair_rows]
        return copy_to(pair, src, u.at[0, (3 * h, 1 + h)[i], body], pair_send.at[6 + i], pair_recv.at[6 + i])

    exchange = [
        kappa_copy(0),
        copy_to(
            pair, kappa_ref.at[:, share((1 - h) * SHIFT + 256, 8)], model.at[own, 256:264], pair_send.at[2], pair_recv.at[2]
        ),
        outer_copy(0),
        outer_copy(1),
        copy_to(pair, now_ref.at[0, 1 - h, pair_rows], u.at[1, 1 + h, body], pair_send.at[3], pair_recv.at[3]),
        kappa_copy(1),
        before_copy(0),
        before_copy(1),
    ]
    direct.start()
    lean[0].start()
    for copy in exchange:
        copy.start()
    band_rows = pl.ds(pl.multiple_of(shot * 16, 8), 16)
    rims = [
        copy_to(next_dom, kappa_ref.at[1, band_rows], kappa_rim.at[0], rim_send.at[0], rim_recv.at[0]),
        copy_to(last_dom, kappa_ref.at[0, band_rows], kappa_rim.at[1], rim_send.at[1], rim_recv.at[1]),
    ]
    for copy in rims:
        copy.start()

    def pass_on(i):
        part = model.at[(3 - 3 * h, 2 - h)[i], eighth]
        for k in range(1, 8):
            copy = copy_to(stack_device(k)[1], part, part, share_send.at[i], share_recv.at[i, z])
            copy.start()

    def take_over(i):
        for k in range(1, 8):
            at, device = stack_device(k)
            part = model.at[(3 - 3 * h, 2 - h)[i], share(at * 32, 32)]
            copy_to(device, part, part, share_send.at[i], share_recv.at[i, at]).wait_recv()

    exchange[0].wait_recv()
    pass_on(0)

    loads[1].wait()
    values = values_seen[0]
    high = values.astype(jnp.bfloat16).astype(jnp.float32)
    low = values - high

    def fill_lanes(i, carry):
        start = pl.multiple_of(i * 16, 16)
        hit = lax.broadcasted_iota(jnp.int32, (16, 2048), 0) + start == lane
        onehot_lanes[pl.ds(start, 16)] = jnp.where(hit, 1.0, 0.0).astype(jnp.bfloat16)
        for n in range(NT):
            onehot_lanes[pl.ds(128 * (1 + n) + start, 16)] = jnp.where(hit, high[n : n + 1], 0.0).astype(jnp.bfloat16)
            onehot_lanes[pl.ds(128 * (5 + n) + start, 16)] = jnp.where(hit, low[n : n + 1], 0.0).astype(jnp.bfloat16)
        return carry

    lax.fori_loop(0, 8, fill_lanes, 0)

    def spread(i, carry):
        start = pl.multiple_of(i * TILE, 16)
        product = lax.dot_general(
            onehot_rows[pl.ds(start, TILE)], onehot_lanes[...], (((1,), (1,)), ((), ())),
            preferred_element_type=jnp.float32,
        )
        counts[0, pl.ds(start, TILE)] = product[:, 0:128]
        for n in range(NT):
            counts[1 + n, pl.ds(start, TILE)] = (
                product[:, 128 * (1 + n) : 128 * (2 + n)] + product[:, 128 * (5 + n) : 128 * (6 + n)]
            )
        return carry

    for i in range(2):
        exchange[2 + i].wait_recv()
        opening[i].start()
    lax.fori_loop(0, EARLY, spread, 0)
    exchange[5].wait_recv()
    pass_on(1)

    spot = source_ref[0]
    spot_plane = lax.shift_right_logical(spot, 16) - PLANES * slab
    spot_row = lax.bitwise_and(lax.shift_right_logical(spot, 7), 511) - SHIFT * h
    spot_lane = lax.bitwise_and(spot, 127)
    lanes = lax.broadcasted_iota(jnp.int32, (BLOCK, 128), 1)
    block_rows = lax.broadcasted_iota(jnp.int32, (BLOCK, 128), 0)
    first_lane = lanes == 0
    last_lane = lanes == 127

    def laplace(field, rim, p, r):
        middle = field[p, pl.ds(PAD + r, BLOCK)]
        if p < PLANES - 1:
            after = field[p + 1, pl.ds(PAD + r, BLOCK)]
        else:
            after = jnp.where(has_above, rim[1][pl.ds(r, BLOCK)], 0.0)
        if p > 0:
            prior = field[p - 1, pl.ds(PAD + r, BLOCK)]
        else:
            prior = jnp.where(has_below, rim[0][pl.ds(r, BLOCK)], 0.0)
        total = after + prior
        total = total + field[p, pl.ds(PAD + 1 + r, BLOCK)] + field[p, pl.ds(PAD - 1 + r, BLOCK)]
        total = total + jnp.where(last_lane, 0.0, pltpu.roll(middle, 127, 1))
        total = total + jnp.where(first_lane, 0.0, pltpu.roll(middle, 1, 1))
        return total - 6.0 * middle, middle

    def rims_of(n):
        if n == 2:
            return near.at[0, pl.ds(PAD, ROWS)], near.at[1, pl.ds(PAD, ROWS)]
        return halo.at[n, 0], halo.at[n, 1]

    def edge(first, size):
        def block(i, carry):
            r = pl.multiple_of(first + i * BLOCK, 8)
            for side in range(2):
                middle = near[side, pl.ds(PAD + r, BLOCK)]
                total = far[side, pl.ds(r, BLOCK)] + u[3, 3 * side, pl.ds(PAD + r, BLOCK)]
                total = total + near[side, pl.ds(PAD + 1 + r, BLOCK)] + near[side, pl.ds(PAD - 1 + r, BLOCK)]
                total = total + jnp.where(last_lane, 0.0, pltpu.roll(middle, 127, 1))
                total = total + jnp.where(first_lane, 0.0, pltpu.roll(middle, 1, 1))
                lap = total - 6.0 * middle
                hit = (spot_plane == 5 * side - 1) & (spot_lane == lanes) & (spot_row - r == block_rows)
                pulse = jnp.where(hit, wavelet_ref[0, 2], 0.0)
                halo[3, side, pl.ds(r, BLOCK)] = (
                    2.0 * middle - halo[1, side, pl.ds(r, BLOCK)] + model_rim[side, pl.ds(r, BLOCK)] * lap + pulse
                )
            return carry

        lax.fori_loop(0, size // BLOCK, block, 0)

    def forward(n, planes, first, size):
        def block(i, carry):
            r = pl.multiple_of(first + i * BLOCK, 8)
            for p in planes:
                lap, middle = laplace(u.at[n + 1], rims_of(n), p, r)
                speed = model[p, pl.ds(r, BLOCK)]
                pulse = jnp.where(
                    (spot_plane == p) & (spot_lane == lanes) & (spot_row - r == block_rows), wavelet_ref[0, n], 0.0
                )
                after = 2.0 * middle - u[n, p, pl.ds(PAD + r, BLOCK)] + speed * lap + pulse
                u[n + 2, p, pl.ds(PAD + r, BLOCK)] = after
                if n < NT - 1:
                    laps[n, p, pl.ds(r, BLOCK)] = lap
                else:
                    miss = counts[0, pl.ds(p * ROWS + r, BLOCK)] * after - counts[NT, pl.ds(p * ROWS + r, BLOCK)]
                    adjoint[0, p, pl.ds(r, BLOCK)] = miss
                    weighted[0, p, pl.ds(PAD + r, BLOCK)] = speed * miss
                    image[int(p in OUTER), p // 2, pl.ds(r, BLOCK)] = miss * lap
            return carry

        lax.fori_loop(0, size // BLOCK, block, 0)

    def backward(j, planes, first, size):
        level = NT - 1 - j

        def block(i, carry):
            r = pl.multiple_of(first + i * BLOCK, 8)
            for p in planes:
                lap, _ = laplace(weighted.at[j], rims_of(NT + j), p, r)
                at = pl.ds(p * ROWS + r, BLOCK)
                miss = counts[0, at] * u[level + 1, p, pl.ds(PAD + r, BLOCK)] - counts[level, at]
                field = 2.0 * adjoint[j, p, pl.ds(r, BLOCK)] + lap + miss
                if j > 0:
                    field = field - adjoint[j - 1, p, pl.ds(r, BLOCK)]
                image[int(p in OUTER), p // 2, pl.ds(r, BLOCK)] += field * laps[level - 1, p, pl.ds(r, BLOCK)]
                if level > 1:
                    adjoint[j + 1, p, pl.ds(r, BLOCK)] = field
                    weighted[j + 1, p, pl.ds(PAD + r, BLOCK)] = model[p, pl.ds(r, BLOCK)] * field
            return carry

        lax.fori_loop(0, size // BLOCK, block, 0)

    def rim_copies(field, n, c):
        first, size = LAGGED[c] if n >= NT else CHUNKS[c]
        at, to = pl.ds(PAD + first, size), pl.ds(first, size)
        into = (near.at[0, at], near.at[1, at]) if n == 2 else (halo.at[n, 0, to], halo.at[n, 1, to])
        return (
            copy_to(above, field.at[PLANES - 1, at], into[0], halo_send.at[n], halo_recv.at[n, c, 0]),
            copy_to(below, field.at[0, at], into[1], halo_send.at[n], halo_recv.at[n, c, 1]),
        )

    def far_copies(i):
        first, size = HALVES[i]
        at, to = pl.ds(PAD + first, size), pl.ds(first, size)
        return (
            copy_to(above, u.at[3, 2, at], far.at[0, to], far_send.at[i, 0], far_recv.at[i, 0]),
            copy_to(below, u.at[3, 1, at], far.at[1, to], far_send.at[i, 1], far_recv.at[i, 1]),
        )

    halos = []

    def send_rims(field, n, c):
        for copy in rim_copies(field, n, c):
            copy.start()

    for load in loads[2:]:
        load.wait()
    for i in (4, 1, 6):
        exchange[i].wait_recv()
    take_over(0)
    for copy in opening:
        copy.wait_recv()

    for c, (first, size) in enumerate(CHUNKS):
        forward(0, OUTER, first, size)
        send_rims(u.at[2], 1, c)
    lean[1].start()
    exchange[7].wait_recv()
    take_over(1)
    forward(0, INNER, 0, ROWS)

    forward(1, INNER, 0, ROWS)
    for i in range(2):
        for copy in far_copies(i):
            copy.start()
            halos.append(copy)
    lax.fori_loop(EARLY, CELL_ROWS // TILE, spread, 0)
    for c, (first, size) in enumerate(CHUNKS):
        for copy in rim_copies(u.at[2], 1, c):
            copy.wait_recv()
        forward(1, OUTER, first, size)
        send_rims(u.at[3], 2, c)

    forward(2, INNER, 0, ROWS)
    for copy in lean:
        copy.wait_recv()
    for i in range(2):
        for copy in far_copies(i):
            copy.wait_recv()
    for c, (first, size) in enumerate(CHUNKS):
        for copy in rim_copies(u.at[3], 2, c):
            copy.wait_recv()
        forward(2, OUTER, first, size)
        edge(*LAGGED[c])
        forward(3, OUTER, *LAGGED[c])
        send_rims(weighted.at[0], NT, c)
    forward(3, INNER, 0, ROWS)

    half = pl.ds(pl.multiple_of(h * 256, 8), 256)
    kept = pl.ds(pl.multiple_of(PAD + 8 * h, 8), 256)
    store = pltpu.make_async_copy(u.at[NT + 1, own, kept], next_ref.at[0, :, half], next_sem.at[0])
    give = copy_to(pair, u.at[NT + 1, theirs, kept], next_ref.at[0, :, half], next_sem.at[1], next_sem.at[2])
    store.start()
    give.start()

    def band(j, parity):
        return pl.ds(pl.multiple_of(8 * h + 16 * (2 * j + parity), 8), 16)

    def core_copy(part, j):
        return copy_to(
            twin, image.at[part, :, band(j, 1 - core)], mate.at[part, j], core_send.at[part, j], core_recv.at[part, j]
        )

    def core_start(part):
        def step(j, carry):
            core_copy(part, j).start()
            return carry

        lax.fori_loop(0, 8, step, 0)

    def ring_copy(part, k):
        at, device = ring_device(k)
        src = shared.at[part, at // 2, lax.rem(at, 2)]
        return copy_to(device, src, crossed.at[part, x], ring_send.at[part, k], ring_recv.at[part, x])

    def core_finish(part):
        def step(j, carry):
            core_copy(part, j).wait_recv()
            shared[part, :, lax.rem(j, 2), j // 2] = image[part, :, band(j, core)] + mate[part, j]
            return carry

        lax.fori_loop(0, 8, step, 0)
        for k in range(1, 4):
            ring_copy(part, k).start()
        crossed[part, x] = shared[part, h, x_lo]

    def stack_copy(part, k):
        at, device = stack_device(k)
        return copy_to(device, gathered.at[part, at], landed.at[part, z], band_send.at[part, k], band_recv.at[part, z])

    def ring_finish(part):
        for k in range(1, 4):
            at, _ = ring_device(k)
            copy_to(twin, crossed.at[part, at], crossed.at[part, at], ring_send.at[part, k], ring_recv.at[part, at]).wait_recv()

        def step(j, carry):
            gathered[part, j] = crossed[part, 0, j] + crossed[part, 1, j]
            gathered[part, 4 + j] = crossed[part, 2, j] + crossed[part, 3, j]
            return carry

        lax.fori_loop(0, 4, step, 0)
        for k in range(1, 8):
            stack_copy(part, k).start()
        landed[part, z] = gathered[part, z]

    def stack_finish(part):
        for k in range(1, 8):
            at, _ = stack_device(k)
            copy_to(twin, landed.at[part, at], landed.at[part, at], band_send.at[part, k], band_recv.at[part, at]).wait_recv()
        total = landed[part, 0]
        for j in range(1, 8):
            total = total + landed[part, j]
        plane_at = h if part else 1 - h
        gradient_ref[plane_at] = total / NT - gradient_ref[plane_at]

    for j in range(NT - 1):
        backward(j, INNER, 0, ROWS)
        if j == NT - 2:
            core_start(0)
            core_finish(0)
        for c, (first, size) in enumerate(LAGGED):
            for copy in rim_copies(weighted.at[j], NT + j, c):
                copy.wait_recv()
            backward(j, OUTER, first, size)
            if j < NT - 2:
                send_rims(weighted.at[j + 1], NT + j + 1, c)
    core_start(1)
    ring_finish(0)
    core_finish(1)

    for copy in rims:
        copy.wait_recv()

    band_lanes = lax.broadcasted_iota(jnp.int32, (16, 128), 1)
    start = pl.multiple_of(PAD + shot * 16, 8)
    for p in range(2):
        middle = kappa_rows[p, pl.ds(start, 16)]
        if p == 0:
            after = kappa_rows[1, pl.ds(start, 16)]
            prior = jnp.where(dom > 0, kappa_rim[0], 0.0)
        else:
            after = jnp.where(dom < 15, kappa_rim[1], 0.0)
            prior = kappa_rows[0, pl.ds(start, 16)]
        total = after + prior
        total = total + kappa_rows[p, pl.ds(start + 1, 16)] + kappa_rows[p, pl.ds(start - 1, 16)]
        total = total + jnp.where(band_lanes == 127, 0.0, pltpu.roll(middle, 127, 1))
        total = total + jnp.where(band_lanes == 0, 0.0, pltpu.roll(middle, 1, 1))
        gradient_ref[p] = (total / 6.0 - middle) * PRIOR_GAIN

    def sent(part):
        def step(j, carry):
            core_copy(part, j).wait_send()
            return carry

        lax.fori_loop(0, 8, step, 0)
        for k in range(1, 4):
            ring_copy(part, k).wait_send()

    for copy in exchange + opening + lean + rims + halos:
        copy.wait_send()
    for n in (1, 2, 4, 5, 6):
        copy_to(twin, halo.at[n], halo.at[n], halo_send.at[n], halo_recv.at[n, 0, 0]).wait_send()
    for i in range(2):
        rows = model.at[0, 0:224]
        copy_to(twin, rows, rows, share_send.at[i], share_recv.at[i, 0]).wait_send()
    store.wait()
    give.wait()
    sent(0)

    ring_finish(1)
    stack_finish(0)
    sent(1)
    for k in range(1, 8):
        stack_copy(0, k).wait_send()
    stack_finish(1)
    for k in range(1, 8):
        stack_copy(1, k).wait_send()


def hand_over(gradient_ref, next_ref, gradient_out, next_out, gradient, waves, load_sem, store_sem):
    loads, stores = [], []
    for p in range(2):
        for i in range(PIECES):
            rows = pl.ds(i * (512 // PIECES), 512 // PIECES)
            at = 1 + p * PIECES + i
            loads.append(pltpu.make_async_copy(next_ref.at[0, p, rows], waves.at[p, rows], load_sem.at[at]))
            stores.append(pltpu.make_async_copy(waves.at[p, rows], next_out.at[0, p, rows], store_sem.at[at]))
    loads.append(pltpu.make_async_copy(gradient_ref, gradient, load_sem.at[0]))
    stores.append(pltpu.make_async_copy(gradient, gradient_out, store_sem.at[0]))
    for load in loads:
        load.start()
    for load, store in zip(loads, stores):
        load.wait()
        store.start()
    for store in stores:
        store.wait()


def shards(kappa, wave_now, wave_before, wavelet, source_cell, receiver_cells, observed):
    f32 = jnp.float32
    chunks = len(CHUNKS)
    anywhere = pl.BlockSpec(memory_space=pl.ANY)
    vmem = pl.BlockSpec(memory_space=pltpu.VMEM)
    smem = pl.BlockSpec(memory_space=pltpu.SMEM)
    dma = pltpu.SemaphoreType.DMA
    results = pl.pallas_call(
        kernel,
        out_shape=(
            jax.ShapeDtypeStruct((2, 16, 128), f32),
            jax.ShapeDtypeStruct(wave_now.shape, f32),
        ),
        in_specs=[anywhere, anywhere, anywhere, smem, smem, anywhere, anywhere],
        out_specs=(vmem, anywhere),
        scratch_shapes=[
            pltpu.VMEM((6, PLANES, ROWS + 2 * PAD, 128), f32),
            pltpu.VMEM((PLANES, ROWS, 128), f32),
            pltpu.VMEM((3, PLANES, ROWS, 128), f32),
            pltpu.VMEM((5, CELL_ROWS, 128), f32),
            pltpu.VMEM((3, PLANES, ROWS, 128), f32),
            pltpu.VMEM((3, PLANES, ROWS + 2 * PAD, 128), f32),
            pltpu.VMEM((7, 2, ROWS, 128), f32),
            pltpu.VMEM((2, ROWS + 2 * PAD, 128), f32),
            pltpu.VMEM((2, ROWS, 128), f32),
            pltpu.VMEM((2, ROWS, 128), f32),
            pltpu.VMEM((2, 2, ROWS, 128), f32),
            pltpu.VMEM((1, 2048), jnp.int32),
            pltpu.VMEM((1, NT, 2048), f32),
            pltpu.VMEM((CELL_ROWS, 2048), jnp.bfloat16),
            pltpu.VMEM((COLUMNS, 2048), jnp.bfloat16),
            pltpu.VMEM((2, 512 + 2 * PAD, 128), f32),
            pltpu.VMEM((2, 16, 128), f32),
            pltpu.VMEM((2, 8, 2, 16, 128), f32),
            pltpu.VMEM((2, 2, 2, 4, 16, 128), f32),
            pltpu.VMEM((2, 4, 4, 16, 128), f32),
            pltpu.VMEM((2, 8, 16, 128), f32),
            pltpu.VMEM((2, 8, 16, 128), f32),
            dma((6,)),
            dma((8,)),
            dma((8,)),
            dma((2,)),
            dma((2, 8)),
            dma((3,)),
            dma((3,)),
            dma((2,)),
            dma((2,)),
            dma((2, 2)),
            dma((2, 2)),
            dma((2,)),
            dma((2,)),
            dma((7,)),
            dma((7, chunks, 2)),
            dma((3,)),
            dma((2, 8)),
            dma((2, 8)),
            dma((2, 4)),
            dma((2, 4)),
            dma((2, 8)),
            dma((2, 8)),
        ],
        name="window",
        compiler_params=pltpu.CompilerParams(
            collective_id=0, has_side_effects=True, vmem_limit_bytes=56 << 20
        ),
    )(kappa, wave_now, wave_before, wavelet, source_cell, receiver_cells, observed)
    return pl.pallas_call(
        hand_over,
        out_shape=tuple(jax.ShapeDtypeStruct(r.shape, r.dtype) for r in results),
        in_specs=[anywhere, anywhere],
        out_specs=(anywhere, anywhere),
        scratch_shapes=[
            pltpu.VMEM((2, 16, 128), f32),
            pltpu.VMEM((2, 512, 128), f32),
            dma((1 + 2 * PIECES,)),
            dma((1 + 2 * PIECES,)),
        ],
        name="hand_over",
    )(*results)


def solution(mesh):
    return jax.shard_map(
        shards,
        mesh=mesh,
        in_specs=(
            P("dom", None, None),
            P("shot", "dom", None, None),
            P("shot", "dom", None, None),
            P("shot", None),
            P("shot"),
            P("shot", None),
            P("shot", None, None),
        ),
        out_specs=(P("dom", "shot", None), P("shot", "dom", None, None)),
        check_vma=False,
    )
```
